256 devices in a mesh: row: 32 (over z, y_lo, core), col: 8 (over y_hi, x).
Axes of the slice: x: 4, y: 4 (y_hi: 2, y_lo: 2; y = y_hi * 2 + y_lo), z: 8, core: 2. Of those that a mesh axis runs over, the one named last changes fastest.
Arguments:
- queries: bfloat16 [256, 256, 2240], P('row', 'col'), may hold values from -6 to 6
- keys: bfloat16 [256, 256, 2240], P('row', 'col'), may hold values from -120 to 120
- values: bfloat16 [256, 256, 2240], P('row', 'col'), may hold values from -10 to 10
- features: bfloat16 [256, 256, 11200], P('row', 'col'), may hold values from -6 to 6
- conv_weight: bfloat16 [3, 3, 11200], replicated, may hold values from -2 to 2
- conv_bias: bfloat16 [11200], replicated, may hold values from -3 to 3
Outputs:
- attended: bfloat16 [256, 256, 2240], P('row', 'col')
- gated: bfloat16 [256, 256, 5600], P('row', 'col')
The draws below stay inside these ranges and needn't reach their ends.
All inputs are finite; a program needn't handle non-finite values.
Results may differ from the reference program's by a relative error of at most 0.001.
Values may be sent and summed in bfloat16 or wider, within the bound.
A program may use at most 128 MiB of HBM per device.

```python
import math
import jax
import jax.numpy as jnp
from jax import lax

D = 2240
HEADS = 70
HEAD_DIM = 32
HID = 5600
TILE_R = 8
TILE_C = 32
IMG_H = 256
IMG_W = 256


def draw_keys(key, part):
    noise_key, scale_key = jax.random.split(key, 2)
    pick_key = jax.random.fold_in(key, 77)
    full_shape = (IMG_H, IMG_W, D)
    tile_count = IMG_H // TILE_R * (IMG_W // TILE_C)
    strong_tile = jax.random.randint(pick_key, (), 0, tile_count)
    tile_index = (jnp.arange(IMG_H, dtype=jnp.int32) // TILE_R).reshape(IMG_H, 1, 1) * (IMG_W // TILE_C) + (jnp.arange(IMG_W, dtype=jnp.int32) // TILE_C).reshape(1, IMG_W, 1)
    tile_weight = jnp.where(tile_index == strong_tile, 1.0, 0.02).astype(jnp.float32)
    row_place = jnp.arange(IMG_H, dtype=jnp.float32).reshape(IMG_H, 1, 1) / (IMG_H - 1)
    noise_part = jnp.clip(jax.random.normal(noise_key, full_shape, jnp.float32), -6.0, 6.0)
    row_rise = 1.0 + 2.0 * row_place
    magnitude = jnp.exp(jax.random.uniform(scale_key, (IMG_H, IMG_W, 1), jnp.float32) * math.log(10.0))
    return (noise_part * magnitude * row_rise * tile_weight / 3.0).astype(jnp.bfloat16)


def draw_values(key, part):
    mean_key, shift_key, noise_key = jax.random.split(key, 3)
    full_shape = (IMG_H, IMG_W, D)
    channel_mean = jnp.clip(jax.random.normal(mean_key, (D,), jnp.float32), -3.0, 3.0)
    tile_shift = jnp.clip(jax.random.normal(shift_key, (IMG_H // TILE_R, IMG_W // TILE_C, D), jnp.float32), -3.0, 3.0)
    tile_shift = jnp.repeat(jnp.repeat(tile_shift, TILE_R, axis=0), TILE_C, axis=1)
    noise_part = jnp.clip(jax.random.normal(noise_key, full_shape, jnp.float32), -4.0, 4.0)
    result = channel_mean + tile_shift + noise_part
    return result.astype(jnp.bfloat16)


def shard_levels(own_key, shape, cuts, smallest, top_value):
    loudness = 1.0
    for position, parts in cuts:
        draws = jax.random.uniform(jax.random.fold_in(jax.random.fold_in(own_key, 6), position), (parts,), jnp.float32, smallest / len(cuts), top_value / len(cuts))
        loudness = loudness * jnp.repeat(jnp.exp(draws), shape[position] // parts).reshape((-1,) + (1,) * (len(shape) - 1 - position))
    return loudness


def scatter_about(own_key, shape, scale, limit, shards=(), held_as=jnp.bfloat16):
    drawn = jax.random.normal(own_key, shape, jnp.float32) * scale
    if len(shards) > 0:
        drawn = shard_levels(own_key, shape, shards, -0.22, 0.18) * drawn
    return jnp.clip(drawn, min=-limit, max=limit).astype(held_as)


def setup_inputs(seed: int = 0) -> dict:
    seeds = jax.random.split(jax.random.key(seed), 7)
    queries = scatter_about(seeds[0], (IMG_H, IMG_W, D), 1.0, 6.0, ((0, 32), (1, 8)))
    keys = draw_keys(jax.random.fold_in(seeds[6], 71), 0)
    values = draw_values(jax.random.fold_in(seeds[6], 71), 0)
    features = scatter_about(seeds[3], (IMG_H, IMG_W, 2 * HID), 1.0, 6.0, ((0, 32), (1, 8)))
    conv_weight = scatter_about(seeds[4], (3, 3, 2 * HID), 9 ** -0.5, 2.0)
    conv_bias = scatter_about(seeds[5], (2 * HID,), 0.5, 3.0)
    return dict(queries=queries, keys=keys, values=values, features=features, conv_weight=conv_weight, conv_bias=conv_bias)


def reference(queries, keys, values, features, conv_weight, conv_bias):
    def add_row(running, row_pair):
        key_row, value_row = row_pair
        key_heads = jnp.maximum(key_row.astype(jnp.float32), 0.0).reshape(-1, HEADS, HEAD_DIM)
        value_heads = value_row.astype(jnp.float32).reshape(-1, HEADS, HEAD_DIM)
        kv_sum, key_sum = running
        kv_sum = kv_sum + jnp.einsum("thj,thi->jhi", value_heads, key_heads)
        key_sum = key_sum + jnp.sum(key_heads, axis=0)
        return (kv_sum, key_sum), None

    initial = (jnp.zeros((HEAD_DIM, HEADS, HEAD_DIM), jnp.float32), jnp.zeros((HEADS, HEAD_DIM), jnp.float32))
    (kv_state, key_total), ignored = lax.scan(add_row, initial, (keys, values))

    def attend_row(query_row):
        query_heads = jnp.maximum(query_row.astype(jnp.float32), 0.0).reshape(-1, HEADS, HEAD_DIM)
        numerator = jnp.einsum("thi,jhi->thj", query_heads, kv_state, precision=lax.Precision.HIGHEST)
        denominator = jnp.einsum("thi,hi->th", query_heads, key_total, precision=lax.Precision.HIGHEST)
        return (numerator / (denominator[:, :, None] + 1e-15)).astype(jnp.bfloat16).reshape(IMG_W, D)

    attended = lax.map(attend_row, queries)

    padded = jnp.pad(features, ((1, 1), (1, 1), (0, 0)))
    weight_float = conv_weight.astype(jnp.float32)
    bias_float = conv_bias.astype(jnp.float32)

    def conv_row(row_index):
        band_rows = lax.dynamic_slice_in_dim(padded, row_index, 3, 0).astype(jnp.float32)
        conv_sum = bias_float
        for tap_row in range(3):
            for tap_col in range(3):
                conv_sum = conv_sum + weight_float[tap_row, tap_col] * band_rows[tap_row, tap_col:tap_col + IMG_W]
        return (conv_sum[:, :HID] * jax.nn.silu(conv_sum[:, HID:])).astype(jnp.bfloat16)

    gated = lax.map(conv_row, jnp.arange(IMG_H, dtype=jnp.int32))
    return attended, gated
```

```python
import functools

import jax
import jax.numpy as jnp
from jax import lax
from jax.experimental import pallas as pl
from jax.experimental.pallas import tpu as pltpu
from jax.sharding import PartitionSpec as P

MESH = pl.DeviceIdType.MESH
F32 = jnp.float32
BF16 = jnp.bfloat16

HEAD_DIM = 32
HID = 5600
LANES = 128
BLOCKS = 18
TILES = 80
HALF = TILES // 2
QUARTER = HALF // 4
OWNERS = 5
SHARE = QUARTER // OWNERS
GATE_TILE = HID // LANES
GATE_SHIFT = LANES - HID % LANES


def iota(shape, dim):
    return lax.broadcasted_iota(jnp.int32, shape, dim)


def position():
    row, col = lax.axis_index("row"), lax.axis_index("col")
    core = lax.rem(row, 2)
    y = lax.div(col, 4) * 2 + lax.rem(lax.div(row, 2), 2)
    return row, col, core, lax.rem(col, 4), y, lax.div(row, 4)


def device(core, x, y, z):
    return (z * 4 + lax.rem(y, 2) * 2 + core, lax.div(y, 2) * 4 + x)


def mix_kernel(
    k_hbm, v_hbm, x_hbm, w_hbm, b_hbm,
    state_hbm, gated_hbm,
    kbuf, vbuf, xbuf, wbuf, bbuf, gbuf,
    up, down, left, right, send_left, send_right,
    corner_in, corner_out, prev, prev_edge,
    part, recv_core, recv_x, recv_z, recv_y, total,
    load_sem, store_sem, halo_send, halo_recv, edge_send, edge_recv, corner_send, corner_recv,
    core_send, core_recv, x_send, x_recv, z_send, z_recv, y_send, y_recv,
):
    row, col, core, x, y, z = position()
    rows, cols, channels = xbuf.shape
    n_row, n_col = lax.axis_size("row"), lax.axis_size("col")
    owner = z < OWNERS

    loads = [
        pltpu.make_async_copy(src, dst, load_sem.at[i])
        for i, (src, dst) in enumerate(
            [(x_hbm, xbuf), (k_hbm, kbuf), (v_hbm, vbuf), (w_hbm, wbuf), (b_hbm, bbuf)]
        )
    ]
    for load in loads:
        load.start()

    has_up, has_down = row > 0, row < n_row - 1
    has_left, has_right = col > 0, col < n_col - 1
    diagonals = [
        (0, has_up & has_left, -1, -1),
        (1, has_up & has_right, -1, 1),
        (2, has_down & has_left, 1, -1),
        (3, has_down & has_right, 1, 1),
    ]

    barrier = pltpu.get_barrier_semaphore()

    def greet(target):
        pl.semaphore_signal(barrier, inc=1, device_id=target, device_id_type=MESH)

    core_mate = device(1 - core, x, y, z)
    x_mates = [device(core, lax.rem(x + d, 4), y, z) for d in range(1, 4)]
    y_mates = [device(core, x, lax.rem(y + d, 4), z) for d in range(1, 4)]
    z_mates = [device(core, x, y, lax.rem(z + d, 8)) for d in range(1, 8)]
    for mate in [core_mate] + x_mates + y_mates + z_mates:
        greet(mate)
    sides = [(has_up, (row - 1, col)), (has_down, (row + 1, col)), (has_left, (row, col - 1)), (has_right, (row, col + 1))]
    for there, target in sides + [(t, (row + a, col + b)) for _, t, a, b in diagonals]:
        pl.when(there)(functools.partial(greet, target))

    @pl.when(row == 0)
    def _():
        up[...] = jnp.zeros_like(up)

    @pl.when(row == n_row - 1)
    def _():
        down[...] = jnp.zeros_like(down)

    @pl.when(col == 0)
    def _():
        left[...] = jnp.zeros_like(left)

    @pl.when(col == n_col - 1)
    def _():
        right[...] = jnp.zeros_like(right)

    for i, there, _, _ in diagonals:
        @pl.when(jnp.logical_not(there))
        def _():
            corner_in[i] = jnp.zeros_like(corner_in[i])

    one = jnp.int32(1)
    up_n, down_n = jnp.minimum(row, one), jnp.minimum(n_row - 1 - row, one)
    left_n, right_n = jnp.minimum(col, one), jnp.minimum(n_col - 1 - col, one)
    pl.semaphore_wait(barrier, 14 + (1 + up_n + down_n) * (1 + left_n + right_n) - 1)

    def remote(src, dst, send, recv, target):
        return pltpu.make_async_remote_copy(
            src_ref=src, dst_ref=dst, send_sem=send, recv_sem=recv, device_id=target, device_id_type=MESH
        )

    to_up = remote(x_hbm.at[0], down, halo_send.at[0], halo_recv.at[0], (row - 1, col))
    to_down = remote(x_hbm.at[rows - 1], up, halo_send.at[1], halo_recv.at[1], (row + 1, col))
    pl.when(has_up)(to_up.start)
    pl.when(has_down)(to_down.start)

    i8 = iota((8, LANES), 0)
    lane = iota((8, LANES), 1)

    loads[0].wait()

    def edge_tile(lanes, width):
        row_id = iota((8, width), 0)
        low = high = jnp.zeros((8, width), F32)
        for r in range(rows):
            first = xbuf[r, 0:16, lanes].astype(F32)[0:1]
            last = xbuf[r, cols - 16 : cols, lanes].astype(F32)[15:16]
            if r in (0, rows - 1):
                place = 0 if r == 0 else 2
                corner_out[place, :, lanes] = first
                corner_out[place + 1, :, lanes] = last
            low = jnp.where(row_id == r, first, low)
            high = jnp.where(row_id == r, last, high)
        send_left[:, lanes] = low.astype(BF16)
        send_right[:, lanes] = high.astype(BF16)

    full_tiles = channels // LANES
    tail = channels - full_tiles * LANES

    @pl.loop(0, full_tiles)
    def _(t):
        edge_tile(pl.ds(pl.multiple_of(t * LANES, LANES), LANES), LANES)

    edge_tile(slice(full_tiles * LANES, channels), tail)

    to_left = remote(send_left, right, edge_send.at[0], edge_recv.at[0], (row, col - 1))
    to_right = remote(send_right, left, edge_send.at[1], edge_recv.at[1], (row, col + 1))
    pl.when(has_left)(to_left.start)
    pl.when(has_right)(to_right.start)
    to_corner = [
        remote(corner_out.at[i], corner_in.at[3 - i], corner_send.at[i], corner_recv.at[3 - i], (row + a, col + b))
        for i, _, a, b in diagonals
    ]
    for i, there, _, _ in diagonals:
        pl.when(there)(to_corner[i].start)

    loads[1].wait()
    loads[2].wait()
    ones = jnp.ones((rows * cols, LANES), BF16)
    sums = [jnp.zeros((8, LANES), F32)] * 4
    for block in range(BLOCKS):
        start = block * LANES
        width = min(LANES, kbuf.shape[2] - start)
        keys = jnp.maximum(kbuf[:, :, start : start + width], 0).reshape(rows * cols, width)
        values = vbuf[:, :, start : start + width].reshape(rows * cols, width)
        contract = (((0,), (0,)), ((), ()))
        if width == LANES:
            both = lax.dot_general(
                keys, jnp.concatenate([values, ones], axis=1), contract, preferred_element_type=F32
            )
            state, key_sum = both[:, :LANES], both[:, LANES:]
        else:
            state = lax.dot_general(keys, values, contract, preferred_element_type=F32)
            state = jnp.concatenate([state, jnp.zeros((width, LANES - width), F32)], axis=1)
            key_sum = lax.dot_general(keys, ones, contract, preferred_element_type=F32)
        heads = width // HEAD_DIM
        for group in range(4):
            tile = jnp.zeros((8, LANES), F32)
            for h in range(heads):
                at = slice(h * HEAD_DIM + group * 8, h * HEAD_DIM + group * 8 + 8)
                tile = jnp.where(lax.div(lane, HEAD_DIM) == h, state[at], tile)
                sums[group] = jnp.where(lane == block * 4 + h, key_sum[at], sums[group])
            part[block * 4 + group] = tile
    for group in range(4):
        part[BLOCKS * 4 + group] = sums[group]
        part[BLOCKS * 4 + 4 + group] = jnp.zeros((8, LANES), F32)

    mine_core, mine_x = core * HALF, core * HALF + x * QUARTER
    mine_z = mine_x + z * SHARE
    add_core = remote(
        part.at[pl.ds((1 - core) * HALF, HALF)], recv_core, core_send.at[0], core_recv.at[0], core_mate
    )
    add_x = [
        remote(
            part.at[pl.ds(core * HALF + lax.rem(x + d, 4) * QUARTER, QUARTER)],
            recv_x.at[d - 1], x_send.at[d - 1], x_recv.at[d - 1], x_mates[d - 1],
        )
        for d in range(1, 4)
    ]

    def owned(d):
        return mine_x + jnp.minimum(lax.rem(z + d, 8), OWNERS - 1) * SHARE

    def owns(d):
        return lax.rem(z + d, 8) < OWNERS

    add_z = [
        remote(
            part.at[pl.ds(owned(d), SHARE)], recv_z.at[d - 1],
            z_send.at[d - 1], z_recv.at[d - 1], z_mates[d - 1],
        )
        for d in range(1, 8)
    ]
    own = pl.ds(owned(0), SHARE)
    add_y = [
        remote(part.at[own], recv_y.at[d - 1], y_send.at[d - 1], y_recv.at[d - 1], y_mates[d - 1])
        for d in range(1, 4)
    ]
    give_z = [
        remote(total.at[own], total.at[own], z_send.at[6 + d], z_recv.at[6 + d], z_mates[d - 1])
        for d in range(1, 8)
    ]
    get_z = [
        remote(
            total.at[pl.ds(owned(8 - d), SHARE)], total.at[pl.ds(owned(8 - d), SHARE)],
            z_send.at[6 + d], z_recv.at[6 + d], z_mates[d - 1],
        )
        for d in range(1, 8)
    ]
    all_x = pl.ds(mine_x, QUARTER)
    give_x = [
        remote(total.at[all_x], total.at[all_x], x_send.at[2 + d], x_recv.at[2 + d], x_mates[d - 1])
        for d in range(1, 4)
    ]
    get_x = [
        remote(
            total.at[pl.ds(core * HALF + lax.rem(x + 4 - d, 4) * QUARTER, QUARTER)],
            total.at[pl.ds(core * HALF + lax.rem(x + 4 - d, 4) * QUARTER, QUARTER)],
            x_send.at[2 + d], x_recv.at[2 + d], x_mates[d - 1],
        )
        for d in range(1, 4)
    ]
    all_core = pl.ds(mine_core, HALF)
    other_core = pl.ds((1 - core) * HALF, HALF)
    give_core = remote(total.at[all_core], total.at[all_core], core_send.at[1], core_recv.at[1], core_mate)
    get_core = remote(total.at[other_core], total.at[other_core], core_send.at[1], core_recv.at[1], core_mate)

    add_core.start()

    def sum_core():
        add_core.wait_recv()
        part[all_core] = part[all_core] + recv_core[...]
        for copy in add_x:
            copy.start()

    def sum_x():
        for copy in add_x:
            copy.wait_recv()
        part[all_x] = part[all_x] + recv_x[0] + recv_x[1] + recv_x[2]
        for d in range(1, 8):
            pl.when(owns(d))(add_z[d - 1].start)

    def sum_z():
        @pl.when(owner)
        def _():
            for copy in add_z:
                copy.wait_recv()
            got = part[own]
            for d in range(7):
                got = got + recv_z[d]
            part[own] = got
            for copy in add_y:
                copy.start()

    def sum_y():
        @pl.when(owner)
        def _():
            for copy in add_y:
                copy.wait_recv()
            total[own] = part[own] + recv_y[0] + recv_y[1] + recv_y[2]
            for copy in give_z:
                copy.start()

    def share_z():
        for d in range(1, 8):
            pl.when(owns(8 - d))(get_z[d - 1].wait_recv)
        for copy in give_x:
            copy.start()

    def share_x():
        for copy in get_x:
            copy.wait_recv()
        give_core.start()

    loads[3].wait()
    loads[4].wait()
    pl.when(has_right)(to_left.wait_recv)
    pl.when(has_left)(to_right.wait_recv)

    def conv(lanes, width, out_rows, fetch, low, high):
        weight = [wbuf[a, :, lanes].astype(F32) for a in range(3)]
        weight = [[weight[a][b : b + 1] for b in range(3)] for a in range(3)]
        bias = bbuf[:, lanes].astype(F32)
        sub = iota((8, width), 0)
        sources = {}
        for r in out_rows:
            for a in (-1, 0, 1):
                if r + a not in sources:
                    sources[r + a] = fetch(r + a)
        results = []
        for r in out_rows:
            around = [sources[r - 1], sources[r], sources[r + 1]]
            taps = []
            for b in range(3):
                taps.append(weight[0][b] * around[0] + weight[1][b] * around[1] + weight[2][b] * around[2])
            middle = taps[1] + bias
            groups = cols // 8
            from_low = [pltpu.roll(taps[0][8 * g : 8 * g + 8], 1, axis=0) for g in range(groups)]
            from_high = [pltpu.roll(taps[2][8 * g : 8 * g + 8], 7, axis=0) for g in range(groups)]
            low_edge = jnp.broadcast_to(
                sum(weight[a][0] * low(r + a - 1) for a in range(3)), (8, width))
            high_edge = jnp.broadcast_to(
                sum(weight[a][2] * high(r + a - 1) for a in range(3)), (8, width))
            out = []
            for g in range(groups):
                before = from_low[g - 1] if g else low_edge
                after = from_high[g + 1] if g + 1 < groups else high_edge
                out.append(
                    middle[8 * g : 8 * g + 8]
                    + jnp.where(sub == 0, before, from_low[g])
                    + jnp.where(sub == 7, after, from_high[g])
                )
            results.append(out)
        return results

    def silu(v):
        half = 0.5 * v
        return half + half * jnp.tanh(half)

    def sources_at(lanes):
        def fetch(r):
            if r < 0:
                return up[:, lanes].astype(F32)
            if r >= rows:
                return down[:, lanes].astype(F32)
            return xbuf[r, :, lanes].astype(F32)

        low_rows = left[:, lanes].astype(F32)
        high_rows = right[:, lanes].astype(F32)

        def low(r):
            if r < 0:
                return corner_in[0, :, lanes]
            return corner_in[2, :, lanes] if r >= rows else low_rows[r : r + 1]

        def high(r):
            if r < 0:
                return corner_in[1, :, lanes]
            return corner_in[3, :, lanes] if r >= rows else high_rows[r : r + 1]

        return fetch, low, high

    def gate_of(lanes, width, out_rows):
        turned = []
        for per_row in conv(lanes, width, out_rows, *sources_at(lanes)):
            for v in per_row:
                v = silu(v)
                if width < LANES:
                    v = jnp.concatenate([v, jnp.zeros((8, LANES - width), F32)], axis=1)
                turned.append(pltpu.roll(v, GATE_SHIFT, axis=1))
        return turned

    def gate_tile(u, out_rows, carry, last=False):
        start = u * LANES if last else pl.multiple_of(u * LANES, LANES)
        lanes = pl.ds(start, LANES)
        value = conv(lanes, LANES, out_rows, *sources_at(lanes))
        if last:
            gate_lanes, width = slice(full_tiles * LANES, channels), tail
        else:
            gate_lanes, width = pl.ds(pl.multiple_of((u + GATE_TILE + 1) * LANES, LANES), LANES), LANES
        turned = gate_of(gate_lanes, width, out_rows)
        for i, r in enumerate(out_rows):
            for pair in range(cols // 16):
                halves = []
                for g in (2 * pair, 2 * pair + 1):
                    at = i * (cols // 8) + g
                    gate = jnp.where(lane < GATE_SHIFT, carry[at], turned[at])
                    carry[at] = turned[at]
                    halves.append(value[i][g] * gate)
                out = jnp.concatenate(halves, axis=0).astype(BF16)
                if last:
                    gbuf[r, 16 * pair : 16 * pair + 16, u * LANES : HID] = out[:, : HID - u * LANES]
                else:
                    gbuf[r, 16 * pair : 16 * pair + 16, lanes] = out

    def all_tiles(out_rows, carry, steps):
        for at, v in enumerate(gate_of(slice(GATE_TILE * LANES, GATE_TILE * LANES + LANES), LANES, out_rows)):
            carry[at] = v

        @pl.loop(0, GATE_TILE)
        def _(u):
            gate_tile(u, out_rows, carry)
            for at, step in steps:
                pl.when(u == at)(step)

        gate_tile(GATE_TILE, out_rows, carry, last=True)

    inner = list(range(1, rows - 1))
    all_tiles(inner, prev, [(8, sum_core), (18, sum_x), (28, sum_z), (38, sum_y)])
    store_inner = pltpu.make_async_copy(
        gbuf.at[pl.ds(1, rows - 2)], gated_hbm.at[pl.ds(1, rows - 2)], store_sem.at[0]
    )
    store_inner.start()
    share_z()
    share_x()
    get_core.wait_recv()
    store_state = pltpu.make_async_copy(total, state_hbm, store_sem.at[1])
    store_state.start()

    pl.when(has_down)(to_up.wait_recv)
    pl.when(has_up)(to_down.wait_recv)
    for i, there, _, _ in diagonals:
        pl.when(there)(to_corner[3 - i].wait_recv)
    all_tiles([0, rows - 1], prev_edge, [])
    store_first = pltpu.make_async_copy(gbuf.at[0], gated_hbm.at[0], store_sem.at[2])
    store_last = pltpu.make_async_copy(gbuf.at[rows - 1], gated_hbm.at[rows - 1], store_sem.at[3])
    store_first.start()
    store_last.start()

    pl.when(has_up)(to_up.wait_send)
    pl.when(has_down)(to_down.wait_send)
    pl.when(has_left)(to_left.wait_send)
    pl.when(has_right)(to_right.wait_send)
    for i, there, _, _ in diagonals:
        pl.when(there)(to_corner[i].wait_send)
    for copy in [add_core, give_core] + add_x + give_x:
        copy.wait_send()
    for d in range(1, 8):
        pl.when(owns(d))(add_z[d - 1].wait_send)

    @pl.when(owner)
    def _():
        for copy in add_y + give_z:
            copy.wait_send()

    for store in [store_inner, store_state, store_first, store_last]:
        store.wait()


def mix(keys, values, features, conv_weight, conv_bias):
    rows, cols, channels = features.shape
    width = keys.shape[2]
    sem = pltpu.SemaphoreType.DMA
    tiles = lambda *lead: pltpu.VMEM(lead + (8, LANES), F32)
    anywhere = pl.BlockSpec(memory_space=pl.ANY)
    return pl.pallas_call(
        mix_kernel,
        name="mix",
        out_shape=(
            jax.ShapeDtypeStruct((TILES, 8, LANES), F32),
            jax.ShapeDtypeStruct((rows, cols, HID), BF16),
        ),
        in_specs=[anywhere] * 5,
        out_specs=[anywhere] * 2,
        scratch_shapes=[
            pltpu.VMEM((rows, cols, width), BF16),
            pltpu.VMEM((rows, cols, width), BF16),
            pltpu.VMEM((rows, cols, channels), BF16),
            pltpu.VMEM((3, 3, channels), BF16),
            pltpu.VMEM((1, channels), BF16),
            pltpu.VMEM((rows, cols, HID), BF16),
            pltpu.VMEM((cols, channels), BF16),
            pltpu.VMEM((cols, channels), BF16),
            pltpu.VMEM((rows, channels), BF16),
            pltpu.VMEM((rows, channels), BF16),
            pltpu.VMEM((rows, channels), BF16),
            pltpu.VMEM((rows, channels), BF16),
            pltpu.VMEM((4, 1, channels), F32),
            pltpu.VMEM((4, 1, channels), F32),
            tiles((rows - 2) * cols // 8),
            tiles(2 * cols // 8),
            tiles(TILES),
            tiles(HALF),
            tiles(3, QUARTER),
            tiles(7, SHARE),
            tiles(3, SHARE),
            tiles(TILES),
            sem((5,)), sem((4,)), sem((2,)), sem((2,)), sem((2,)), sem((2,)), sem((4,)), sem((4,)),
            sem((2,)), sem((2,)), sem((6,)), sem((6,)), sem((14,)), sem((14,)), sem((3,)), sem((3,)),
        ],
        compiler_params=pltpu.CompilerParams(
            collective_id=0, has_side_effects=True, vmem_limit_bytes=48 << 20
        ),
        cost_estimate=pl.CostEstimate(flops=100_000_000, bytes_accessed=12_000_000, transcendentals=1_500_000),
    )(keys, values, features, conv_weight, conv_bias.reshape(1, channels))


def attend_kernel(q_hbm, state, mixed_hbm, attended_hbm, gated_hbm, qbuf, abuf, matrix, sem):
    rows, cols, width = qbuf.shape
    move = pltpu.make_async_copy(mixed_hbm, gated_hbm, sem.at[0])
    load = pltpu.make_async_copy(q_hbm, qbuf, sem.at[1])
    load.start()
    move.start()

    lane = iota((HEAD_DIM, LANES), 1)
    head_of_lane = lax.div(lane, HEAD_DIM)

    def split(v):
        high = v.astype(BF16)
        return high, (v - high.astype(F32)).astype(BF16)

    sum_high, sum_low = split(state[pl.ds(BLOCKS * 4, 4)].reshape(HEAD_DIM, LANES))

    def block_diagonal(v):
        v = v.astype(F32)
        return jnp.concatenate([jnp.where(head_of_lane == h, v, 0.0) for h in range(4)], axis=0).astype(BF16)

    def build(block):
        high, low = split(state[pl.ds(block * 4, 4)].reshape(HEAD_DIM, LANES))
        picks = (iota((LANES, LANES), 0) == block * 4 + lax.div(iota((LANES, LANES), 1), HEAD_DIM))
        picks = picks.astype(F32).astype(BF16)
        key_high = jnp.dot(sum_high, picks, preferred_element_type=F32)
        key_low = jnp.dot(sum_low, picks, preferred_element_type=F32)
        top = jnp.concatenate([block_diagonal(high), block_diagonal(key_high)], axis=1)
        bottom = jnp.concatenate([block_diagonal(low), block_diagonal(key_low)], axis=1)
        matrix[block] = jnp.concatenate([top, bottom], axis=0)

    for block in range(BLOCKS):
        build(block)
    load.wait()
    for block in range(BLOCKS):
        start = block * LANES
        size = min(LANES, width - start)
        queries = jnp.maximum(qbuf[:, :, start : start + size], 0).reshape(rows * cols, size)
        if size < LANES:
            queries = jnp.concatenate([queries, jnp.zeros((rows * cols, LANES - size), BF16)], axis=1)
        both = jnp.dot(jnp.concatenate([queries, queries], axis=1), matrix[block], preferred_element_type=F32)
        out = (both[:, :LANES] / (both[:, LANES:] + 1e-15)).astype(BF16).reshape(rows, cols, LANES)
        abuf[:, :, start : start + size] = out[:, :, :size]
    store = pltpu.make_async_copy(abuf, attended_hbm, sem.at[2])
    store.start()
    store.wait()
    move.wait()


def attend(queries, state, mixed):
    anywhere = pl.BlockSpec(memory_space=pl.ANY)
    return pl.pallas_call(
        attend_kernel,
        name="attend",
        out_shape=(
            jax.ShapeDtypeStruct(queries.shape, BF16),
            jax.ShapeDtypeStruct(mixed.shape, BF16),
        ),
        in_specs=[anywhere, pl.BlockSpec(memory_space=pltpu.VMEM), anywhere],
        out_specs=[anywhere] * 2,
        scratch_shapes=[
            pltpu.VMEM(queries.shape, BF16),
            pltpu.VMEM(queries.shape, BF16),
            pltpu.VMEM((BLOCKS, 2 * LANES, 2 * LANES), BF16),
            pltpu.SemaphoreType.DMA((3,)),
        ],
        compiler_params=pltpu.CompilerParams(vmem_limit_bytes=32 << 20),
        cost_estimate=pl.CostEstimate(flops=600_000_000, bytes_accessed=8_000_000, transcendentals=0),
    )(queries, state, mixed)


def on_device(queries, keys, values, features, conv_weight, conv_bias):
    state, mixed = mix(keys, values, features, conv_weight, conv_bias)
    return attend(queries, state, mixed)


def solution(mesh):
    return jax.shard_map(
        on_device,
        mesh=mesh,
        in_specs=(
            P("row", "col", None),
            P("row", "col", None),
            P("row", "col", None),
            P("row", "col", None),
            P(),
            P(),
        ),
        out_specs=(P("row", "col", None), P("row", "col", None)),
        check_vma=False,
    )
```

```python
import functools

import jax
import jax.numpy as jnp
from jax import lax
from jax.experimental import pallas as pl
from jax.experimental.pallas import tpu as pltpu
from jax.sharding import PartitionSpec as P

MESH = pl.DeviceIdType.MESH
F32 = jnp.float32
BF16 = jnp.bfloat16

HEAD_DIM = 32
HID = 5600
LANES = 128
BLOCKS = 18
USED = 10
QUARTER = 12
SHARE = QUARTER // 4
HALF = 4 * QUARTER
TILES = 2 * HALF
GATE_TILE = HID // LANES
GATE_SHIFT = LANES - HID % LANES
CHUNK = 4
CHUNKS = 11
DEPTH = 2
STEP_AT = (4, 18, 28, 41)


def slot(tile):
    return tile // USED * QUARTER + tile % USED


def iota(shape, dim):
    return lax.broadcasted_iota(jnp.int32, shape, dim)


def position():
    row, col = lax.axis_index("row"), lax.axis_index("col")
    core = lax.rem(row, 2)
    y = lax.div(col, 4) * 2 + lax.rem(lax.div(row, 2), 2)
    return row, col, core, lax.rem(col, 4), y, lax.div(row, 4)


def device(core, x, y, z):
    return (z * 4 + lax.rem(y, 2) * 2 + core, lax.div(y, 2) * 4 + x)


def mix_kernel(
    k_hbm, v_hbm, x_hbm, w_hbm, b_hbm,
    state_hbm, gated_hbm,
    kbuf, vbuf, xbuf, wbuf, bbuf, gbuf,
    halo, left, right, send_left, send_right,
    corner_in, corner_out, tail_in, tail_out, prev, gates,
    part, recv_core, recv_x, recv_z, recv_y, total,
    load_sem, store_sem, halo_send, halo_recv, mate_send, mate_recv, edge_send, edge_recv, corner_send, corner_recv,
    core_send, core_recv, x_send, x_recv, z_send, z_recv, y_send, y_recv,
):
    row, col, core, x, y, z = position()
    rows, cols, channels = xbuf.shape
    n_row, n_col = lax.axis_size("row"), lax.axis_size("col")

    loads = [
        pltpu.make_async_copy(src, dst, load_sem.at[i])
        for i, (src, dst) in enumerate(
            [(k_hbm, kbuf), (v_hbm, vbuf), (x_hbm, xbuf), (w_hbm, wbuf), (b_hbm, bbuf)]
        )
    ]
    for load in loads:
        load.start()

    has_up, has_down = row > 0, row < n_row - 1
    has_left, has_right = col > 0, col < n_col - 1
    diagonals = [
        (0, has_up & has_left, -1, -1),
        (1, has_up & has_right, -1, 1),
        (2, has_down & has_left, 1, -1),
        (3, has_down & has_right, 1, 1),
    ]

    barrier = pltpu.get_barrier_semaphore()

    def greet(target):
        pl.semaphore_signal(barrier, inc=1, device_id=target, device_id_type=MESH)

    core_mate = device(1 - core, x, y, z)
    x_mates = [device(core, lax.rem(x + d, 4), y, z) for d in range(1, 4)]
    y_mates = [device(core, x, lax.rem(y + d, 4), z) for d in range(1, 4)]
    z_mates = [device(core, x, y, lax.rem(z + d, 8)) for d in range(1, 8)]
    for mate in [core_mate] + x_mates + y_mates + z_mates:
        greet(mate)
    sides = [(has_up, (row - 1, col)), (has_down, (row + 1, col)), (has_left, (row, col - 1)), (has_right, (row, col + 1))]
    for there, target in sides + [(t, (row + a, col + b)) for _, t, a, b in diagonals]:
        pl.when(there)(functools.partial(greet, target))

    crosses = (row + core > 0) & (row + core < n_row)

    @pl.when(jnp.logical_not(crosses))
    def _():
        halo[core] = jnp.zeros_like(halo[core])

    @pl.when(col == 0)
    def _():
        left[...] = jnp.zeros_like(left)

    @pl.when(col == n_col - 1)
    def _():
        right[...] = jnp.zeros_like(right)

    for i, there, _, _ in diagonals:
        @pl.when(jnp.logical_not(there))
        def _():
            corner_in[i] = jnp.zeros_like(corner_in[i])

    one = jnp.int32(1)
    up_n, down_n = jnp.minimum(row, one), jnp.minimum(n_row - 1 - row, one)
    left_n, right_n = jnp.minimum(col, one), jnp.minimum(n_col - 1 - col, one)
    pl.semaphore_wait(barrier, 14 + (1 + up_n + down_n) * (1 + left_n + right_n) - 1)

    def remote(src, dst, send, recv, target):
        return pltpu.make_async_remote_copy(
            src_ref=src, dst_ref=dst, send_sem=send, recv_sem=recv, device_id=target, device_id_type=MESH
        )

    full_tiles = channels // LANES
    tail = channels - full_tiles * LANES
    mate_row = remote(x_hbm.at[(1 - core) * (rows - 1)], halo.at[core], mate_send.at[0], mate_recv.at[0], core_mate)
    far_row = x_hbm.at[core * (rows - 1)]
    far_target = (row + 2 * core - 1, col)
    mate_row.start()

    def chunk(at):
        copies = []
        for part_of in range(2):
            first, count = at * CHUNK + part_of * (GATE_TILE + 1), CHUNK
            if isinstance(at, int):
                count = min(CHUNK, full_tiles - first)
            lanes = pl.ds(pl.multiple_of(first * LANES, LANES), count * LANES)
            copies.append(remote(
                far_row.at[:, lanes], halo.at[1 - core, :, lanes],
                halo_send.at[part_of, at], halo_recv.at[part_of, at], far_target,
            ))
        return copies

    def start_chunk(at):
        @pl.when(crosses)
        def _():
            for copy in chunk(at):
                copy.start()

    def sent_chunk(at):
        @pl.when(crosses)
        def _():
            for copy in chunk(at):
                copy.wait_send()

    def received_chunk(at):
        @pl.when(crosses)
        def _():
            for copy in chunk(at):
                copy.wait_recv()

    def advance(step):
        if step >= DEPTH:
            sent_chunk(order[step - DEPTH])
        if step < CHUNKS:
            start_chunk(order[step])

    order = [CHUNKS - 1] + list(range(CHUNKS - 1))
    advance(0)

    lane = iota((8, LANES), 1)

    loads[0].wait()
    loads[1].wait()
    ones = jnp.ones((rows * cols, LANES), BF16)
    sums = [jnp.zeros((8, LANES), F32)] * 4
    for block in range(BLOCKS):
        start = block * LANES
        width = min(LANES, kbuf.shape[2] - start)
        keys = jnp.maximum(kbuf[:, :, start : start + width], 0).reshape(rows * cols, width)
        values = vbuf[:, :, start : start + width].reshape(rows * cols, width)
        contract = (((0,), (0,)), ((), ()))
        if width == LANES:
            both = lax.dot_general(
                keys, jnp.concatenate([values, ones], axis=1), contract, preferred_element_type=F32
            )
            state, key_sum = both[:, :LANES], both[:, LANES:]
        else:
            state = lax.dot_general(keys, values, contract, preferred_element_type=F32)
            state = jnp.concatenate([state, jnp.zeros((width, LANES - width), F32)], axis=1)
            key_sum = lax.dot_general(keys, ones, contract, preferred_element_type=F32)
        heads = width // HEAD_DIM
        for group in range(4):
            tile = jnp.zeros((8, LANES), F32)
            for h in range(heads):
                at = slice(h * HEAD_DIM + group * 8, h * HEAD_DIM + group * 8 + 8)
                tile = jnp.where(lax.div(lane, HEAD_DIM) == h, state[at], tile)
                sums[group] = jnp.where(lane == block * 4 + h, key_sum[at], sums[group])
            part[slot(block * 4 + group)] = tile
    for group in range(4):
        part[slot(BLOCKS * 4 + group)] = sums[group]
        part[slot(BLOCKS * 4 + 4 + group)] = jnp.zeros((8, LANES), F32)
    for quarter in range(8):
        for unused in range(USED, QUARTER):
            part[quarter * QUARTER + unused] = jnp.zeros((8, LANES), F32)

    def quarter(at, size=USED):
        return pl.ds(core * HALF + at * QUARTER, size)

    def share(at):
        return pl.ds(core * HALF + x * QUARTER + at * SHARE, SHARE)

    def ring(at, d, n):
        return lax.rem(at + d + n, n)

    mine_half, other_half = pl.ds(core * HALF, HALF), pl.ds((1 - core) * HALF, HALF)
    mine_x, mine_y = quarter(x), share(y)
    add_core = remote(part.at[other_half], recv_core, core_send.at[0], core_recv.at[0], core_mate)
    add_x, add_y, add_z, give_x, give_y, get_x, get_y = [], [], [], [], [], [], []
    for d in range(1, 4):
        a, b = d - 1, d + 2
        add_x.append(remote(part.at[quarter(ring(x, d, 4))], recv_x.at[a], x_send.at[a], x_recv.at[a], x_mates[a]))
        add_y.append(remote(part.at[share(ring(y, d, 4))], recv_y.at[a], y_send.at[a], y_recv.at[a], y_mates[a]))
        give_x.append(remote(total.at[mine_x], total.at[mine_x], x_send.at[b], x_recv.at[b], x_mates[a]))
        give_y.append(remote(total.at[mine_y], total.at[mine_y], y_send.at[b], y_recv.at[b], y_mates[a]))
        from_x, from_y = quarter(ring(x, -d, 4)), share(ring(y, -d, 4))
        get_x.append(remote(total.at[from_x], total.at[from_x], x_send.at[b], x_recv.at[b], x_mates[a]))
        get_y.append(remote(total.at[from_y], total.at[from_y], y_send.at[b], y_recv.at[b], y_mates[a]))
    for d in range(1, 8):
        add_z.append(remote(part.at[mine_y], recv_z.at[d - 1], z_send.at[d - 1], z_recv.at[d - 1], z_mates[d - 1]))
    give_core = remote(total.at[mine_half], total.at[mine_half], core_send.at[1], core_recv.at[1], core_mate)
    get_core = remote(total.at[other_half], total.at[other_half], core_send.at[1], core_recv.at[1], core_mate)

    def start_all(copies):
        for copy in copies:
            copy.start()

    def receive_all(copies):
        for copy in copies:
            copy.wait_recv()

    def sum_core():
        add_core.wait_recv()
        part[mine_half] = part[mine_half] + recv_core[...]
        start_all(add_x)

    def sum_x():
        receive_all(add_x)
        part[mine_x] = part[mine_x] + recv_x[0] + recv_x[1] + recv_x[2]
        start_all(add_y)

    def sum_y():
        receive_all(add_y)
        part[mine_y] = part[mine_y] + recv_y[0] + recv_y[1] + recv_y[2]
        start_all(add_z)

    def sum_z():
        receive_all(add_z)
        got = part[mine_y]
        for d in range(7):
            got = got + recv_z[d]
        total[mine_y] = got
        start_all(give_y)

    def share_y():
        receive_all(get_y)
        start_all(give_x)

    def share_x():
        receive_all(get_x)
        give_core.start()

    add_core.start()

    loads[2].wait()

    def edge_tile(lanes, width):
        row_id = iota((8, width), 0)
        low = high = jnp.zeros((8, width), F32)
        for r in range(rows):
            first = xbuf[r, 0:16, lanes].astype(F32)[0:1]
            last = xbuf[r, cols - 16 : cols, lanes].astype(F32)[15:16]
            if r in (0, rows - 1):
                place = 0 if r == 0 else 2
                corner_out[place, :, lanes] = first
                corner_out[place + 1, :, lanes] = last
            low = jnp.where(row_id == r, first, low)
            high = jnp.where(row_id == r, last, high)
        send_left[:, lanes] = low.astype(BF16)
        send_right[:, lanes] = high.astype(BF16)

    @pl.loop(0, full_tiles)
    def _(t):
        edge_tile(pl.ds(pl.multiple_of(t * LANES, LANES), LANES), LANES)

    edge_tile(slice(full_tiles * LANES, channels), tail)
    sum_core()
    rest = xbuf[core * (rows - 1), :, full_tiles * LANES :]
    tail_out[...] = jnp.concatenate([rest, jnp.zeros((cols, LANES - tail), BF16)], axis=1)
    far_tail = remote(tail_out, tail_in, mate_send.at[1], mate_recv.at[1], far_target)

    to_left = remote(send_left, right, edge_send.at[0], edge_recv.at[0], (row, col - 1))
    to_right = remote(send_right, left, edge_send.at[1], edge_recv.at[1], (row, col + 1))
    pl.when(has_left)(to_left.start)
    pl.when(has_right)(to_right.start)
    to_corner = [
        remote(corner_out.at[i], corner_in.at[3 - i], corner_send.at[i], corner_recv.at[3 - i], (row + a, col + b))
        for i, _, a, b in diagonals
    ]
    for i, there, _, _ in diagonals:
        pl.when(there)(to_corner[i].start)

    def bias_at(lanes, width):
        return bbuf[:, lanes].astype(F32)

    pl.when(crosses)(far_tail.start)
    advance(1)

    groups = cols // 8

    def conv(lanes, width, out_rows):
        sub = iota((8, width), 0)

        def wide(v):
            return jnp.broadcast_to(v, (8, width))

        weight = []
        for a in range(3):
            taps = wbuf[a, :, lanes].astype(F32)
            weight.append([wide(taps[b : b + 1]) for b in range(3)])
        bias = wide(bias_at(lanes, width))

        def fetch(r):
            source = []
            for at in range(0, cols, 16):
                if r < 0 or r >= rows:
                    pair = halo[int(r >= rows), at : at + 16, lanes]
                else:
                    pair = xbuf[r, at : at + 16, lanes]
                pair = pair.astype(F32)
                source += [pair[:8], pair[8:]]
            return source

        def edge(column, tap, corners):
            middle = column[:, lanes].astype(F32)
            above, below = pltpu.roll(middle, 1, axis=0), pltpu.roll(middle, 7, axis=0)
            if out_rows[0] == 0:
                above = jnp.where(sub == 0, wide(corner_in[corners[0], :, lanes]), above)
                below = jnp.where(sub == 7, wide(corner_in[corners[1], :, lanes]), below)
            return weight[0][tap] * above + weight[1][tap] * middle + weight[2][tap] * below

        low, high = edge(left, 0, (0, 2)), edge(right, 2, (1, 3))
        window = {}
        for r in out_rows:
            window = {a: window[a] if a in window else fetch(a) for a in (r - 1, r, r + 1)}
            before, now, after = window[r - 1], window[r], window[r + 1]
            taps = [
                [weight[0][b] * before[g] + weight[1][b] * now[g] + weight[2][b] * after[g] for g in range(groups)]
                for b in range(3)
            ]
            from_low = [wide(low[r : r + 1])] + [pltpu.roll(v, 1, axis=0) for v in taps[0]]
            from_high = [pltpu.roll(v, 7, axis=0) for v in taps[2]] + [wide(high[r : r + 1])]
            yield [
                (taps[1][g] + bias)
                + jnp.where(sub == 0, from_low[g], from_low[g + 1])
                + jnp.where(sub == 7, from_high[g + 1], from_high[g])
                for g in range(groups)
            ]

    def gate_tile(lanes, width, out_rows, carry):
        at = 0
        for sums_of_row in conv(lanes, width, out_rows):
            for v in sums_of_row:
                half = 0.5 * v
                v = half + half * jnp.tanh(half)
                if width < LANES:
                    v = jnp.concatenate([v, jnp.zeros((8, LANES - width), F32)], axis=1)
                v = pltpu.roll(v, GATE_SHIFT, axis=1)
                gates[at] = jnp.where(lane < GATE_SHIFT, carry[at], v)
                carry[at] = v
                at += 1

    def value_tile(lanes, width, out_rows):
        at = 0
        for r, sums_of_row in zip(out_rows, conv(lanes, LANES, out_rows)):
            for g in range(0, groups, 2):
                out = jnp.concatenate(
                    [sums_of_row[g] * gates[at], sums_of_row[g + 1] * gates[at + 1]], axis=0
                ).astype(BF16)
                if width == LANES:
                    gbuf[r, 8 * g : 8 * g + 16, lanes] = out
                else:
                    gbuf[r, 8 * g : 8 * g + 16, HID - width : HID] = out[:, :width]
                at += 2

    def tile_at(t):
        return pl.ds(pl.multiple_of(t * LANES, LANES), LANES)

    def first_tile(out_rows, carry):
        for at in range(len(out_rows) * groups):
            carry[at] = jnp.zeros((8, LANES), F32)
        gate_tile(slice(GATE_TILE * LANES, GATE_TILE * LANES + LANES), LANES, out_rows, carry)

    def some_tiles(out_rows, carry, begin, end):
        @pl.loop(begin, end)
        def _(u):
            gate_tile(tile_at(u + GATE_TILE + 1), LANES, out_rows, carry)
            value_tile(tile_at(u), LANES, out_rows)

    def last_tile(out_rows, carry):
        gate_tile(slice(full_tiles * LANES, channels), tail, out_rows, carry)
        value_tile(slice(GATE_TILE * LANES, GATE_TILE * LANES + LANES), HID % LANES, out_rows)

    loads[3].wait()
    loads[4].wait()
    sum_x()
    advance(2)
    advance(3)
    pl.when(has_right)(to_left.wait_recv)
    pl.when(has_left)(to_right.wait_recv)
    inner = list(range(1, rows - 1))
    steps = [(sum_y, 4, 5), (sum_z, 6, 7), (share_y, 8, 9), (share_x, 10)]
    first_tile(inner, prev)

    @pl.loop(0, GATE_TILE)
    def _(u):
        for at, (step, *chunks) in zip(STEP_AT, steps):
            @pl.when(u == at)
            def _():
                step()
                for next_chunk in chunks:
                    advance(next_chunk)

        gate_tile(tile_at(u + GATE_TILE + 1), LANES, inner, prev)
        value_tile(tile_at(u), LANES, inner)

    last_tile(inner, prev)
    store_inner = pltpu.make_async_copy(
        gbuf.at[pl.ds(1, rows - 2)], gated_hbm.at[pl.ds(1, rows - 2)], store_sem.at[0]
    )
    store_inner.start()

    received_chunk(CHUNKS - 1)
    mate_row.wait_recv()

    @pl.when(crosses)
    def _():
        far_tail.wait_recv()
        halo[core, :, full_tiles * LANES :] = tail_in[:, :tail]

    for i, there, _, _ in diagonals:
        pl.when(there)(to_corner[3 - i].wait_recv)
    outer = [0, rows - 1]
    first_tile(outer, prev)

    @pl.loop(0, CHUNKS - 1)
    def _(at):
        received_chunk(at)
        some_tiles(outer, prev, at * CHUNK, at * CHUNK + CHUNK)

    some_tiles(outer, prev, (CHUNKS - 1) * CHUNK, GATE_TILE)
    last_tile(outer, prev)
    store_first = pltpu.make_async_copy(gbuf.at[0], gated_hbm.at[0], store_sem.at[2])
    store_last = pltpu.make_async_copy(gbuf.at[rows - 1], gated_hbm.at[rows - 1], store_sem.at[3])
    store_first.start()
    store_last.start()
    get_core.wait_recv()
    store_state = pltpu.make_async_copy(total, state_hbm, store_sem.at[1])
    store_state.start()

    for step in range(CHUNKS, CHUNKS + DEPTH):
        advance(step)
    mate_row.wait_send()
    pl.when(crosses)(far_tail.wait_send)
    pl.when(has_left)(to_left.wait_send)
    pl.when(has_right)(to_right.wait_send)
    for i, there, _, _ in diagonals:
        pl.when(there)(to_corner[i].wait_send)
    for copy in [add_core, give_core] + add_x + add_y + add_z + give_y + give_x:
        copy.wait_send()
    for store in [store_inner, store_state, store_first, store_last]:
        store.wait()


def mix(keys, values, features, conv_weight, conv_bias):
    rows, cols, channels = features.shape
    width = keys.shape[2]
    sem = pltpu.SemaphoreType.DMA
    tiles = lambda *lead: pltpu.VMEM(lead + (8, LANES), F32)
    anywhere = pl.BlockSpec(memory_space=pl.ANY)
    return pl.pallas_call(
        mix_kernel,
        name="mix",
        out_shape=(
            jax.ShapeDtypeStruct((TILES, 8, LANES), F32),
            jax.ShapeDtypeStruct((rows, cols, HID), BF16),
        ),
        in_specs=[pl.BlockSpec(memory_space=pltpu.HBM)] * 5,
        out_specs=[anywhere] * 2,
        scratch_shapes=[
            pltpu.VMEM((rows, cols, width), BF16),
            pltpu.VMEM((rows, cols, width), BF16),
            pltpu.VMEM((rows, cols, channels), BF16),
            pltpu.VMEM((3, 3, channels), BF16),
            pltpu.VMEM((1, channels), BF16),
            pltpu.VMEM((rows, cols, HID), BF16),
            pltpu.VMEM((2, cols, channels), BF16),
            pltpu.VMEM((rows, channels), BF16),
            pltpu.VMEM((rows, channels), BF16),
            pltpu.VMEM((rows, channels), BF16),
            pltpu.VMEM((rows, channels), BF16),
            pltpu.VMEM((4, 1, channels), F32),
            pltpu.VMEM((4, 1, channels), F32),
            pltpu.VMEM((cols, LANES), BF16),
            pltpu.VMEM((cols, LANES), BF16),
            tiles((rows - 2) * cols // 8),
            tiles((rows - 2) * cols // 8),
            tiles(TILES),
            tiles(HALF),
            tiles(3, USED),
            tiles(7, SHARE),
            tiles(3, SHARE),
            tiles(TILES),
            sem((5,)), sem((4,)), sem((2, CHUNKS)), sem((2, CHUNKS)), sem((2,)), sem((2,)),
            sem((2,)), sem((2,)), sem((4,)), sem((4,)),
            sem((2,)), sem((2,)), sem((6,)), sem((6,)), sem((7,)), sem((7,)), sem((6,)), sem((6,)),
        ],
        compiler_params=pltpu.CompilerParams(
            collective_id=0, has_side_effects=True, vmem_limit_bytes=48 << 20
        ),
        cost_estimate=pl.CostEstimate(flops=100_000_000, bytes_accessed=12_000_000, transcendentals=1_500_000),
    )(keys, values, features, conv_weight, conv_bias.reshape(1, channels))


def attend_kernel(q_hbm, state, mixed_hbm, attended_hbm, gated_hbm, qbuf, abuf, matrix, sem):
    rows, cols, width = qbuf.shape
    move = pltpu.make_async_copy(mixed_hbm, gated_hbm, sem.at[0])
    load = pltpu.make_async_copy(q_hbm, qbuf, sem.at[1])
    load.start()
    move.start()

    lane = iota((HEAD_DIM, LANES), 1)
    head_of_lane = lax.div(lane, HEAD_DIM)

    def split(v):
        high = v.astype(BF16)
        return high, (v - high.astype(F32)).astype(BF16)

    def rows_of(block):
        return jnp.concatenate([state[slot(block * 4 + group)] for group in range(4)], axis=0)

    sum_high, sum_low = split(rows_of(BLOCKS))

    def block_diagonal(v):
        v = v.astype(F32)
        return jnp.concatenate([jnp.where(head_of_lane == h, v, 0.0) for h in range(4)], axis=0).astype(BF16)

    def build(block):
        high, low = split(rows_of(block))
        picks = (iota((LANES, LANES), 0) == block * 4 + lax.div(iota((LANES, LANES), 1), HEAD_DIM))
        picks = picks.astype(F32).astype(BF16)
        key_high = jnp.dot(sum_high, picks, preferred_element_type=F32)
        key_low = jnp.dot(sum_low, picks, preferred_element_type=F32)
        top = jnp.concatenate([block_diagonal(high), block_diagonal(key_high)], axis=1)
        bottom = jnp.concatenate([block_diagonal(low), block_diagonal(key_low)], axis=1)
        matrix[block] = jnp.concatenate([top, bottom], axis=0)

    for block in range(BLOCKS):
        build(block)
    load.wait()
    for block in range(BLOCKS):
        start = block * LANES
        size = min(LANES, width - start)
        queries = jnp.maximum(qbuf[:, :, start : start + size], 0).reshape(rows * cols, size)
        if size < LANES:
            queries = jnp.concatenate([queries, jnp.zeros((rows * cols, LANES - size), BF16)], axis=1)
        both = jnp.dot(jnp.concatenate([queries, queries], axis=1), matrix[block], preferred_element_type=F32)
        out = (both[:, :LANES] / (both[:, LANES:] + 1e-15)).astype(BF16).reshape(rows, cols, LANES)
        abuf[:, :, start : start + size] = out[:, :, :size]
    store = pltpu.make_async_copy(abuf, attended_hbm, sem.at[2])
    store.start()
    store.wait()
    move.wait()


def attend(queries, state, mixed):
    anywhere = pl.BlockSpec(memory_space=pl.ANY)
    return pl.pallas_call(
        attend_kernel,
        name="attend",
        out_shape=(
            jax.ShapeDtypeStruct(queries.shape, BF16),
            jax.ShapeDtypeStruct(mixed.shape, BF16),
        ),
        in_specs=[anywhere, pl.BlockSpec(memory_space=pltpu.VMEM), anywhere],
        out_specs=[anywhere] * 2,
        scratch_shapes=[
            pltpu.VMEM(queries.shape, BF16),
            pltpu.VMEM(queries.shape, BF16),
            pltpu.VMEM((BLOCKS, 2 * LANES, 2 * LANES), BF16),
            pltpu.SemaphoreType.DMA((3,)),
        ],
        compiler_params=pltpu.CompilerParams(vmem_limit_bytes=32 << 20),
        cost_estimate=pl.CostEstimate(flops=600_000_000, bytes_accessed=8_000_000, transcendentals=0),
    )(queries, state, mixed)


def on_device(queries, keys, values, features, conv_weight, conv_bias):
    hold = functools.partial(pltpu.with_memory_space_constraint, memory_space=pltpu.HBM)
    keys, values, conv_weight = hold(keys), hold(values), hold(conv_weight)
    state, mixed = mix(keys, values, features, conv_weight, conv_bias)
    return attend(queries, state, mixed)


def solution(mesh):
    return jax.shard_map(
        on_device,
        mesh=mesh,
        in_specs=(
            P("row", "col", None),
            P("row", "col", None),
            P("row", "col", None),
            P("row", "col", None),
            P(),
            P(),
        ),
        out_specs=(P("row", "col", None), P("row", "col", None)),
        check_vma=False,
    )
```

```python
import functools

import jax
import jax.numpy as jnp
from jax import lax
from jax.experimental import pallas as pl
from jax.experimental.pallas import tpu as pltpu
from jax.sharding import PartitionSpec as P

MESH = pl.DeviceIdType.MESH
F32 = jnp.float32
BF16 = jnp.bfloat16

HEAD_DIM = 32
HID = 5600
LANES = 128
BLOCKS = 18
USED = 10
QUARTER = 12
SHARE = QUARTER // 4
HALF = 4 * QUARTER
TILES = 2 * HALF
GATE_TILE = HID // LANES
GATE_SHIFT = LANES - HID % LANES
CHUNK = 4
CHUNKS = 11
FIRST, SECOND = 3,6
SUM_X_AT, SUM_Y_AT, SUM_Z_AT = 24, 42, 30
SHARE_X_AT = 4


def slot(tile):
    return tile // USED * QUARTER + tile % USED


def iota(shape, dim):
    return lax.broadcasted_iota(jnp.int32, shape, dim)


def position():
    row, col = lax.axis_index("row"), lax.axis_index("col")
    core = lax.rem(row, 2)
    y = lax.div(col, 4) * 2 + lax.rem(lax.div(row, 2), 2)
    return row, col, core, lax.rem(col, 4), y, lax.div(row, 4)


def device(core, x, y, z):
    return (z * 4 + lax.rem(y, 2) * 2 + core, lax.div(y, 2) * 4 + x)


def mix_kernel(
    k_hbm, v_hbm, x_hbm, w_hbm, b_hbm,
    state_hbm, gated_hbm,
    kbuf, vbuf, xbuf, wbuf, bbuf, gbuf,
    halo, left, right, send_left, send_right,
    corner_in, corner_out, tail_in, tail_out, prev, gates,
    part, recv_core, recv_x, recv_z, recv_y, total,
    load_sem, store_sem, halo_send, halo_recv, mate_send, mate_recv, edge_send, edge_recv, corner_send, corner_recv,
    core_send, core_recv, x_send, x_recv, z_send, z_recv, y_send, y_recv,
):
    row, col, core, x, y, z = position()
    rows, cols, channels = xbuf.shape
    n_row, n_col = lax.axis_size("row"), lax.axis_size("col")

    loads = [
        pltpu.make_async_copy(src, dst, load_sem.at[i])
        for i, (src, dst) in enumerate(
            [(k_hbm, kbuf), (v_hbm, vbuf), (x_hbm, xbuf), (w_hbm, wbuf), (b_hbm, bbuf)]
        )
    ]
    for load in loads:
        load.start()

    has_up, has_down = row > 0, row < n_row - 1
    has_left, has_right = col > 0, col < n_col - 1
    diagonals = [
        (0, has_up & has_left, -1, -1),
        (1, has_up & has_right, -1, 1),
        (2, has_down & has_left, 1, -1),
        (3, has_down & has_right, 1, 1),
    ]

    barrier = pltpu.get_barrier_semaphore()

    def greet(target):
        pl.semaphore_signal(barrier, inc=1, device_id=target, device_id_type=MESH)

    core_mate = device(1 - core, x, y, z)
    x_mates = [device(core, lax.rem(x + d, 4), y, z) for d in range(1, 4)]
    y_mates = [device(core, x, lax.rem(y + d, 4), z) for d in range(1, 4)]
    z_mates = [device(core, x, y, lax.rem(z + d, 8)) for d in range(1, 8)]
    for mate in [core_mate] + x_mates + y_mates + z_mates:
        greet(mate)
    sides = [(has_up, (row - 1, col)), (has_down, (row + 1, col)), (has_left, (row, col - 1)), (has_right, (row, col + 1))]
    for there, target in sides + [(t, (row + a, col + b)) for _, t, a, b in diagonals]:
        pl.when(there)(functools.partial(greet, target))

    crosses = (row + core > 0) & (row + core < n_row)

    @pl.when(jnp.logical_not(crosses))
    def _():
        halo[core] = jnp.zeros_like(halo[core])

    @pl.when(col == 0)
    def _():
        left[...] = jnp.zeros_like(left)

    @pl.when(col == n_col - 1)
    def _():
        right[...] = jnp.zeros_like(right)

    for i, there, _, _ in diagonals:
        @pl.when(jnp.logical_not(there))
        def _():
            corner_in[i] = jnp.zeros_like(corner_in[i])

    one = jnp.int32(1)
    up_n, down_n = jnp.minimum(row, one), jnp.minimum(n_row - 1 - row, one)
    left_n, right_n = jnp.minimum(col, one), jnp.minimum(n_col - 1 - col, one)
    pl.semaphore_wait(barrier, 14 + (1 + up_n + down_n) * (1 + left_n + right_n) - 1)

    def remote(src, dst, send, recv, target):
        return pltpu.make_async_remote_copy(
            src_ref=src, dst_ref=dst, send_sem=send, recv_sem=recv, device_id=target, device_id_type=MESH
        )

    full_tiles = channels // LANES
    tail = channels - full_tiles * LANES
    mate_row = remote(x_hbm.at[(1 - core) * (rows - 1)], halo.at[core], mate_send.at[0], mate_recv.at[0], core_mate)
    far_row = x_hbm.at[core * (rows - 1)]
    far_target = (row + 2 * core - 1, col)
    mate_row.start()

    def chunk(at):
        copies = []
        for part_of in range(2):
            first, count = at * CHUNK + part_of * (GATE_TILE + 1), CHUNK
            if isinstance(at, int):
                count = min(CHUNK, full_tiles - first)
            lanes = pl.ds(pl.multiple_of(first * LANES, LANES), count * LANES)
            copies.append(remote(
                far_row.at[:, lanes], halo.at[1 - core, :, lanes],
                halo_send.at[part_of, at], halo_recv.at[part_of, at], far_target,
            ))
        return copies

    def start_chunk(at):
        @pl.when(crosses)
        def _():
            for copy in chunk(at):
                copy.start()

    def sent_chunk(at):
        @pl.when(crosses)
        def _():
            for copy in chunk(at):
                copy.wait_send()

    def received_chunk(at):
        @pl.when(crosses)
        def _():
            for copy in chunk(at):
                copy.wait_recv()

    order = [CHUNKS - 1] + list(range(CHUNKS - 1))

    def start_chunks(begin, end):
        for step in range(begin, end):
            start_chunk(order[step])

    start_chunks(0, FIRST)

    lane = iota((8, LANES), 1)

    loads[0].wait()
    loads[1].wait()
    ones = jnp.ones((rows * cols, LANES), BF16)
    sums = [jnp.zeros((8, LANES), F32)] * 4
    for block in range(BLOCKS):
        start = block * LANES
        width = min(LANES, kbuf.shape[2] - start)
        keys = jnp.maximum(kbuf[:, :, start : start + width], 0).reshape(rows * cols, width)
        values = vbuf[:, :, start : start + width].reshape(rows * cols, width)
        contract = (((0,), (0,)), ((), ()))
        if width == LANES:
            both = lax.dot_general(
                keys, jnp.concatenate([values, ones], axis=1), contract, preferred_element_type=F32
            )
            state, key_sum = both[:, :LANES], both[:, LANES:]
        else:
            state = lax.dot_general(keys, values, contract, preferred_element_type=F32)
            state = jnp.concatenate([state, jnp.zeros((width, LANES - width), F32)], axis=1)
            key_sum = lax.dot_general(keys, ones, contract, preferred_element_type=F32)
        heads = width // HEAD_DIM
        for group in range(4):
            tile = jnp.zeros((8, LANES), F32)
            for h in range(heads):
                at = slice(h * HEAD_DIM + group * 8, h * HEAD_DIM + group * 8 + 8)
                tile = jnp.where(lax.div(lane, HEAD_DIM) == h, state[at], tile)
                sums[group] = jnp.where(lane == block * 4 + h, key_sum[at], sums[group])
            part[slot(block * 4 + group)] = tile
    for group in range(4):
        part[slot(BLOCKS * 4 + group)] = sums[group]
        part[slot(BLOCKS * 4 + 4 + group)] = jnp.zeros((8, LANES), F32)
    for quarter in range(8):
        for unused in range(USED, QUARTER):
            part[quarter * QUARTER + unused] = jnp.zeros((8, LANES), F32)

    def quarter(at, size=USED):
        return pl.ds(core * HALF + at * QUARTER, size)

    def share(at):
        return pl.ds(core * HALF + x * QUARTER + at * SHARE, SHARE)

    def ring(at, d, n):
        return lax.rem(at + d + n, n)

    mine_half, other_half = pl.ds(core * HALF, HALF), pl.ds((1 - core) * HALF, HALF)
    mine_x, mine_y = quarter(x), share(y)
    add_core = remote(part.at[other_half], recv_core, core_send.at[0], core_recv.at[0], core_mate)
    add_x, add_y, add_z, give_x, give_y, get_x, get_y = [], [], [], [], [], [], []
    for d in range(1, 4):
        a, b = d - 1, d + 2
        add_x.append(remote(part.at[quarter(ring(x, d, 4))], recv_x.at[a], x_send.at[a], x_recv.at[a], x_mates[a]))
        add_y.append(remote(part.at[share(ring(y, d, 4))], recv_y.at[a], y_send.at[a], y_recv.at[a], y_mates[a]))
        give_x.append(remote(total.at[mine_x], total.at[mine_x], x_send.at[b], x_recv.at[b], x_mates[a]))
        give_y.append(remote(total.at[mine_y], total.at[mine_y], y_send.at[b], y_recv.at[b], y_mates[a]))
        from_x, from_y = quarter(ring(x, -d, 4)), share(ring(y, -d, 4))
        get_x.append(remote(total.at[from_x], total.at[from_x], x_send.at[b], x_recv.at[b], x_mates[a]))
        get_y.append(remote(total.at[from_y], total.at[from_y], y_send.at[b], y_recv.at[b], y_mates[a]))
    for d in range(1, 8):
        add_z.append(remote(part.at[mine_y], recv_z.at[d - 1], z_send.at[d - 1], z_recv.at[d - 1], z_mates[d - 1]))
    give_core = remote(total.at[mine_half], total.at[mine_half], core_send.at[1], core_recv.at[1], core_mate)
    get_core = remote(total.at[other_half], total.at[other_half], core_send.at[1], core_recv.at[1], core_mate)

    def start_all(copies):
        for copy in copies:
            copy.start()

    def receive_all(copies):
        for copy in copies:
            copy.wait_recv()

    def sum_core():
        add_core.wait_recv()
        part[mine_half] = part[mine_half] + recv_core[...]
        start_all(add_x)

    def sum_x():
        receive_all(add_x)
        part[mine_x] = part[mine_x] + recv_x[0] + recv_x[1] + recv_x[2]
        start_all(add_y)

    def sum_y():
        receive_all(add_y)
        part[mine_y] = part[mine_y] + recv_y[0] + recv_y[1] + recv_y[2]
        start_all(add_z)

    def sum_z():
        receive_all(add_z)
        got = part[mine_y]
        for d in range(7):
            got = got + recv_z[d]
        total[mine_y] = got
        start_all(give_y)

    def share_y():
        receive_all(get_y)
        start_all(give_x)

    def share_x():
        receive_all(get_x)
        give_core.start()

    add_core.start()

    loads[2].wait()

    def edge_tile(lanes, width):
        row_id = iota((8, width), 0)
        low = high = jnp.zeros((8, width), F32)
        for r in range(rows):
            first = xbuf[r, 0:16, lanes].astype(F32)[0:1]
            last = xbuf[r, cols - 16 : cols, lanes].astype(F32)[15:16]
            if r in (0, rows - 1):
                place = 0 if r == 0 else 2
                corner_out[place, :, lanes] = first
                corner_out[place + 1, :, lanes] = last
            low = jnp.where(row_id == r, first, low)
            high = jnp.where(row_id == r, last, high)
        send_left[:, lanes] = low.astype(BF16)
        send_right[:, lanes] = high.astype(BF16)

    @pl.loop(0, full_tiles)
    def _(t):
        edge_tile(pl.ds(pl.multiple_of(t * LANES, LANES), LANES), LANES)

    edge_tile(slice(full_tiles * LANES, channels), tail)
    sum_core()
    rest = xbuf[core * (rows - 1), :, full_tiles * LANES :]
    tail_out[...] = jnp.concatenate([rest, jnp.zeros((cols, LANES - tail), BF16)], axis=1)
    far_tail = remote(tail_out, tail_in, mate_send.at[1], mate_recv.at[1], far_target)

    to_left = remote(send_left, right, edge_send.at[0], edge_recv.at[0], (row, col - 1))
    to_right = remote(send_right, left, edge_send.at[1], edge_recv.at[1], (row, col + 1))
    pl.when(has_left)(to_left.start)
    pl.when(has_right)(to_right.start)
    to_corner = [
        remote(corner_out.at[i], corner_in.at[3 - i], corner_send.at[i], corner_recv.at[3 - i], (row + a, col + b))
        for i, _, a, b in diagonals
    ]
    for i, there, _, _ in diagonals:
        pl.when(there)(to_corner[i].start)

    def bias_at(lanes, width):
        return bbuf[:, lanes].astype(F32)

    pl.when(crosses)(far_tail.start)

    groups = cols // 8

    def conv(lanes, width, out_rows, out_groups):
        sub = iota((8, width), 0)

        def wide(v):
            return jnp.broadcast_to(v, (8, width))

        weight = []
        for a in range(3):
            taps = wbuf[a, :, lanes].astype(F32)
            weight.append([wide(taps[b : b + 1]) for b in range(3)])
        bias = wide(bias_at(lanes, width))

        def fetch(r):
            source = []
            for at in range(0, cols, 16):
                if r < 0 or r >= rows:
                    pair = halo[int(r >= rows), at : at + 16, lanes]
                else:
                    pair = xbuf[r, at : at + 16, lanes]
                pair = pair.astype(F32)
                source += [pair[:8], pair[8:]]
            return source

        def edge(column, tap, corners):
            middle = column[:, lanes].astype(F32)
            above, below = pltpu.roll(middle, 1, axis=0), pltpu.roll(middle, 7, axis=0)
            if out_rows[0] == 0:
                above = jnp.where(sub == 0, wide(corner_in[corners[0], :, lanes]), above)
                below = jnp.where(sub == 7, wide(corner_in[corners[1], :, lanes]), below)
            return weight[0][tap] * above + weight[1][tap] * middle + weight[2][tap] * below

        if 0 in out_groups:
            low, high = edge(left, 0, (0, 2)), edge(right, 2, (1, 3))
        window = {}
        for r in out_rows:
            window = {a: window[a] if a in window else fetch(a) for a in (r - 1, r, r + 1)}
            before, now, after = window[r - 1], window[r], window[r + 1]

            def tap(b, g):
                return weight[0][b] * before[g] + weight[1][b] * now[g] + weight[2][b] * after[g]

            from_low, from_high = {}, {}
            for g in range(groups):
                if g in out_groups or g + 1 in out_groups:
                    from_low[g] = pltpu.roll(tap(0, g), 1, axis=0)
                if g in out_groups or g - 1 in out_groups:
                    from_high[g] = pltpu.roll(tap(2, g), 7, axis=0)
            if 0 in out_groups:
                from_low[-1], from_high[groups] = wide(low[r : r + 1]), wide(high[r : r + 1])
            yield [
                (tap(1, g) + bias)
                + jnp.where(sub == 0, from_low[g - 1], from_low[g])
                + jnp.where(sub == 7, from_high[g + 1], from_high[g])
                for g in out_groups
            ]

    def gate_tile(lanes, width, where):
        at = 0
        for sums_of_row in conv(lanes, width, *where):
            for v in sums_of_row:
                half = 0.5 * v
                v = half + half * jnp.tanh(half)
                if width < LANES:
                    v = jnp.concatenate([v, jnp.zeros((8, LANES - width), F32)], axis=1)
                v = pltpu.roll(v, GATE_SHIFT, axis=1)
                gates[at] = jnp.where(lane < GATE_SHIFT, prev[at], v)
                prev[at] = v
                at += 1

    def value_tile(lanes, width, where):
        at = 0
        for r, sums_of_row in zip(where[0], conv(lanes, LANES, *where)):
            for g, v in zip(where[1], sums_of_row):
                out = (v * gates[at]).astype(BF16)
                if width == LANES:
                    gbuf[r, 8 * g : 8 * g + 8, lanes] = out
                else:
                    gbuf[r, 8 * g : 8 * g + 8, HID - width : HID] = out[:, :width]
                at += 1

    def tile_at(t):
        return pl.ds(pl.multiple_of(t * LANES, LANES), LANES)

    def first_tile(where):
        for at in range(len(where[0]) * len(where[1])):
            prev[at] = jnp.zeros((8, LANES), F32)
        gate_tile(slice(GATE_TILE * LANES, GATE_TILE * LANES + LANES), LANES, where)

    def some_tiles(where, begin, end, actions=()):
        @pl.loop(begin, end)
        def _(u):
            for at, action, argument in actions:
                pl.when(u == at)(functools.partial(action, *argument))
            gate_tile(tile_at(u + GATE_TILE + 1), LANES, where)
            value_tile(tile_at(u), LANES, where)

    def last_tile(where):
        gate_tile(slice(full_tiles * LANES, channels), tail, where)
        value_tile(slice(GATE_TILE * LANES, GATE_TILE * LANES + LANES), HID % LANES, where)

    loads[3].wait()
    loads[4].wait()
    where = (list(range(1, rows - 1)), list(range(1, groups - 1)))
    first_tile(where)
    some_tiles(where, 0, GATE_TILE, [
        (SUM_X_AT, sum_x, ()), (SUM_Y_AT, sum_y, ()), (SUM_Y_AT, start_chunks, (FIRST, SECOND)),
    ])
    last_tile(where)

    pl.when(has_right)(to_left.wait_recv)
    pl.when(has_left)(to_right.wait_recv)
    where = (list(range(1, rows - 1)), [0, groups - 1])
    first_tile(where)
    some_tiles(where, 0, GATE_TILE, [(SUM_Z_AT, sum_z, ()), (SUM_Z_AT, start_chunks, (SECOND, CHUNKS))])
    last_tile(where)
    share_y()
    store_inner = pltpu.make_async_copy(
        gbuf.at[pl.ds(1, rows - 2)], gated_hbm.at[pl.ds(1, rows - 2)], store_sem.at[0]
    )
    store_inner.start()

    received_chunk(CHUNKS - 1)
    mate_row.wait_recv()

    @pl.when(crosses)
    def _():
        far_tail.wait_recv()
        halo[core, :, full_tiles * LANES :] = tail_in[:, :tail]

    for i, there, _, _ in diagonals:
        pl.when(there)(to_corner[3 - i].wait_recv)
    where = ([0, rows - 1], list(range(groups)))
    first_tile(where)

    @pl.loop(0, CHUNKS - 1)
    def _(at):
        pl.when(at == SHARE_X_AT)(share_x)
        received_chunk(at)
        some_tiles(where, at * CHUNK, at * CHUNK + CHUNK)

    some_tiles(where, (CHUNKS - 1) * CHUNK, GATE_TILE)
    last_tile(where)
    store_first = pltpu.make_async_copy(gbuf.at[0], gated_hbm.at[0], store_sem.at[2])
    store_last = pltpu.make_async_copy(gbuf.at[rows - 1], gated_hbm.at[rows - 1], store_sem.at[3])
    store_first.start()
    store_last.start()
    get_core.wait_recv()
    store_state = pltpu.make_async_copy(total, state_hbm, store_sem.at[1])
    store_state.start()

    for at in order:
        sent_chunk(at)
    mate_row.wait_send()
    pl.when(crosses)(far_tail.wait_send)
    pl.when(has_left)(to_left.wait_send)
    pl.when(has_right)(to_right.wait_send)
    for i, there, _, _ in diagonals:
        pl.when(there)(to_corner[i].wait_send)
    for copy in [add_core, give_core] + add_x + add_y + add_z + give_y + give_x:
        copy.wait_send()
    for store in [store_inner, store_state, store_first, store_last]:
        store.wait()


def mix(keys, values, features, conv_weight, conv_bias):
    rows, cols, channels = features.shape
    width = keys.shape[2]
    sem = pltpu.SemaphoreType.DMA
    tiles = lambda *lead: pltpu.VMEM(lead + (8, LANES), F32)
    anywhere = pl.BlockSpec(memory_space=pl.ANY)
    return pl.pallas_call(
        mix_kernel,
        name="mix",
        out_shape=(
            jax.ShapeDtypeStruct((TILES, 8, LANES), F32),
            jax.ShapeDtypeStruct((rows, cols, HID), BF16),
        ),
        in_specs=[pl.BlockSpec(memory_space=pltpu.HBM)] * 5,
        out_specs=[anywhere] * 2,
        scratch_shapes=[
            pltpu.VMEM((rows, cols, width), BF16),
            pltpu.VMEM((rows, cols, width), BF16),
            pltpu.VMEM((rows, cols, channels), BF16),
            pltpu.VMEM((3, 3, channels), BF16),
            pltpu.VMEM((1, channels), BF16),
            pltpu.VMEM((rows, cols, HID), BF16),
            pltpu.VMEM((2, cols, channels), BF16),
            pltpu.VMEM((rows, channels), BF16),
            pltpu.VMEM((rows, channels), BF16),
            pltpu.VMEM((rows, channels), BF16),
            pltpu.VMEM((rows, channels), BF16),
            pltpu.VMEM((4, 1, channels), F32),
            pltpu.VMEM((4, 1, channels), F32),
            pltpu.VMEM((cols, LANES), BF16),
            pltpu.VMEM((cols, LANES), BF16),
            tiles((rows - 2) * cols // 8),
            tiles((rows - 2) * cols // 8),
            tiles(TILES),
            tiles(HALF),
            tiles(3, USED),
            tiles(7, SHARE),
            tiles(3, SHARE),
            tiles(TILES),
            sem((5,)), sem((4,)), sem((2, CHUNKS)), sem((2, CHUNKS)), sem((2,)), sem((2,)),
            sem((2,)), sem((2,)), sem((4,)), sem((4,)),
            sem((2,)), sem((2,)), sem((6,)), sem((6,)), sem((7,)), sem((7,)), sem((6,)), sem((6,)),
        ],
        compiler_params=pltpu.CompilerParams(
            collective_id=0, has_side_effects=True, vmem_limit_bytes=48 << 20
        ),
        cost_estimate=pl.CostEstimate(flops=100_000_000, bytes_accessed=12_000_000, transcendentals=1_500_000),
    )(keys, values, features, conv_weight, conv_bias.reshape(1, channels))


def attend_kernel(q_hbm, state, mixed_hbm, attended_hbm, gated_hbm, qbuf, abuf, matrix, sem):
    rows, cols, width = qbuf.shape
    move = pltpu.make_async_copy(mixed_hbm, gated_hbm, sem.at[0])
    load = pltpu.make_async_copy(q_hbm, qbuf, sem.at[1])
    load.start()
    move.start()

    lane = iota((HEAD_DIM, LANES), 1)
    head_of_lane = lax.div(lane, HEAD_DIM)

    def split(v):
        high = v.astype(BF16)
        return high, (v - high.astype(F32)).astype(BF16)

    def rows_of(block):
        return jnp.concatenate([state[slot(block * 4 + group)] for group in range(4)], axis=0)

    sum_high, sum_low = split(rows_of(BLOCKS))

    def block_diagonal(v):
        v = v.astype(F32)
        return jnp.concatenate([jnp.where(head_of_lane == h, v, 0.0) for h in range(4)], axis=0).astype(BF16)

    def build(block):
        high, low = split(rows_of(block))
        picks = (iota((LANES, LANES), 0) == block * 4 + lax.div(iota((LANES, LANES), 1), HEAD_DIM))
        picks = picks.astype(F32).astype(BF16)
        key_high = jnp.dot(sum_high, picks, preferred_element_type=F32)
        key_low = jnp.dot(sum_low, picks, preferred_element_type=F32)
        top = jnp.concatenate([block_diagonal(high), block_diagonal(key_high)], axis=1)
        bottom = jnp.concatenate([block_diagonal(low), block_diagonal(key_low)], axis=1)
        matrix[block] = jnp.concatenate([top, bottom], axis=0)

    for block in range(BLOCKS):
        build(block)
    load.wait()
    for block in range(BLOCKS):
        start = block * LANES
        size = min(LANES, width - start)
        queries = jnp.maximum(qbuf[:, :, start : start + size], 0).reshape(rows * cols, size)
        if size < LANES:
            queries = jnp.concatenate([queries, jnp.zeros((rows * cols, LANES - size), BF16)], axis=1)
        both = jnp.dot(jnp.concatenate([queries, queries], axis=1), matrix[block], preferred_element_type=F32)
        out = (both[:, :LANES] / (both[:, LANES:] + 1e-15)).astype(BF16).reshape(rows, cols, LANES)
        abuf[:, :, start : start + size] = out[:, :, :size]
    store = pltpu.make_async_copy(abuf, attended_hbm, sem.at[2])
    store.start()
    store.wait()
    move.wait()


def attend(queries, state, mixed):
    anywhere = pl.BlockSpec(memory_space=pl.ANY)
    return pl.pallas_call(
        attend_kernel,
        name="attend",
        out_shape=(
            jax.ShapeDtypeStruct(queries.shape, BF16),
            jax.ShapeDtypeStruct(mixed.shape, BF16),
        ),
        in_specs=[anywhere, pl.BlockSpec(memory_space=pltpu.VMEM), anywhere],
        out_specs=[anywhere] * 2,
        scratch_shapes=[
            pltpu.VMEM(queries.shape, BF16),
            pltpu.VMEM(queries.shape, BF16),
            pltpu.VMEM((BLOCKS, 2 * LANES, 2 * LANES), BF16),
            pltpu.SemaphoreType.DMA((3,)),
        ],
        compiler_params=pltpu.CompilerParams(vmem_limit_bytes=32 << 20),
        cost_estimate=pl.CostEstimate(flops=600_000_000, bytes_accessed=8_000_000, transcendentals=0),
    )(queries, state, mixed)


def on_device(queries, keys, values, features, conv_weight, conv_bias):
    hold = functools.partial(pltpu.with_memory_space_constraint, memory_space=pltpu.HBM)
    keys, values, conv_weight = hold(keys), hold(values), hold(conv_weight)
    state, mixed = mix(keys, values, features, conv_weight, conv_bias)
    return attend(queries, state, mixed)


def solution(mesh):
    return jax.shard_map(
        on_device,
        mesh=mesh,
        in_specs=(
            P("row", "col", None),
            P("row", "col", None),
            P("row", "col", None),
            P("row", "col", None),
            P(),
            P(),
        ),
        out_specs=(P("row", "col", None), P("row", "col", None)),
        check_vma=False,
    )
```

```python
import functools

import jax
import jax.numpy as jnp
from jax import lax
from jax.experimental import pallas as pl
from jax.experimental.pallas import tpu as pltpu
from jax.sharding import PartitionSpec as P

MESH = pl.DeviceIdType.MESH
F32 = jnp.float32
BF16 = jnp.bfloat16

HEAD_DIM = 32
HID = 5600
LANES = 128
BLOCKS = 18
USED = 10
QUARTER = 12
SHARE = QUARTER // 4
HALF = 4 * QUARTER
TILES = 2 * HALF
GATE_TILE = HID // LANES
GATE_SHIFT = LANES - HID % LANES
CHUNK = 4
CHUNKS = 11
FIRST, SECOND = 3, 6
SUM_X_AT, SUM_Y_AT, SUM_Z_AT = 24, 40, 28
SHARE_X_AT = 4


def slot(tile):
    return tile // USED * QUARTER + tile % USED


def iota(shape, dim):
    return lax.broadcasted_iota(jnp.int32, shape, dim)


def position():
    row, col = lax.axis_index("row"), lax.axis_index("col")
    core = lax.rem(row, 2)
    y = lax.div(col, 4) * 2 + lax.rem(lax.div(row, 2), 2)
    return row, col, core, lax.rem(col, 4), y, lax.div(row, 4)


def device(core, x, y, z):
    return (z * 4 + lax.rem(y, 2) * 2 + core, lax.div(y, 2) * 4 + x)


def mix_kernel(
    k_hbm, v_hbm, x_hbm, w_hbm, b_hbm,
    state_hbm, gated_hbm,
    kbuf, vbuf, xbuf, wbuf, bbuf, bias_row, gbuf,
    halo, left, right, send_left, send_right,
    corner_in, corner_out, tail_in, tail_out, prev, gates,
    part, recv_core, recv_x, recv_z, recv_y, total,
    load_sem, store_sem, halo_send, halo_recv, mate_send, mate_recv, edge_send, edge_recv, corner_send, corner_recv,
    core_send, core_recv, x_send, x_recv, z_send, z_recv, y_send, y_recv,
):
    row, col, core, x, y, z = position()
    rows, cols, channels = xbuf.shape
    n_row, n_col = lax.axis_size("row"), lax.axis_size("col")

    loads = [
        pltpu.make_async_copy(src, dst, load_sem.at[i])
        for i, (src, dst) in enumerate(
            [(k_hbm, kbuf), (v_hbm, vbuf), (x_hbm, xbuf), (w_hbm, wbuf), (b_hbm, bbuf)]
        )
    ]
    for load in loads:
        load.start()

    has_up, has_down = row > 0, row < n_row - 1
    has_left, has_right = col > 0, col < n_col - 1
    diagonals = [
        (0, has_up & has_left, -1, -1),
        (1, has_up & has_right, -1, 1),
        (2, has_down & has_left, 1, -1),
        (3, has_down & has_right, 1, 1),
    ]

    barrier = pltpu.get_barrier_semaphore()

    def greet(target):
        pl.semaphore_signal(barrier, inc=1, device_id=target, device_id_type=MESH)

    core_mate = device(1 - core, x, y, z)
    x_mates = [device(core, lax.rem(x + d, 4), y, z) for d in range(1, 4)]
    y_mates = [device(core, x, lax.rem(y + d, 4), z) for d in range(1, 4)]
    z_mates = [device(core, x, y, lax.rem(z + d, 8)) for d in range(1, 8)]
    for mate in [core_mate] + x_mates + y_mates + z_mates:
        greet(mate)
    sides = [(has_up, (row - 1, col)), (has_down, (row + 1, col)), (has_left, (row, col - 1)), (has_right, (row, col + 1))]
    for there, target in sides + [(t, (row + a, col + b)) for _, t, a, b in diagonals]:
        pl.when(there)(functools.partial(greet, target))

    crosses = (row + core > 0) & (row + core < n_row)

    @pl.when(jnp.logical_not(crosses))
    def _():
        halo[core] = jnp.zeros_like(halo[core])

    @pl.when(col == 0)
    def _():
        left[...] = jnp.zeros_like(left)

    @pl.when(col == n_col - 1)
    def _():
        right[...] = jnp.zeros_like(right)

    for i, there, _, _ in diagonals:
        @pl.when(jnp.logical_not(there))
        def _():
            corner_in[i] = jnp.zeros_like(corner_in[i])

    one = jnp.int32(1)
    up_n, down_n = jnp.minimum(row, one), jnp.minimum(n_row - 1 - row, one)
    left_n, right_n = jnp.minimum(col, one), jnp.minimum(n_col - 1 - col, one)
    pl.semaphore_wait(barrier, 14 + (1 + up_n + down_n) * (1 + left_n + right_n) - 1)

    def remote(src, dst, send, recv, target):
        return pltpu.make_async_remote_copy(
            src_ref=src, dst_ref=dst, send_sem=send, recv_sem=recv, device_id=target, device_id_type=MESH
        )

    full_tiles = channels // LANES
    tail = channels - full_tiles * LANES
    mate_row = remote(x_hbm.at[(1 - core) * (rows - 1)], halo.at[core], mate_send.at[0], mate_recv.at[0], core_mate)
    far_row = x_hbm.at[core * (rows - 1)]
    far_target = (row + 2 * core - 1, col)
    mate_row.start()

    def chunk(at):
        copies = []
        for part_of in range(2):
            first, count = at * CHUNK + part_of * (GATE_TILE + 1), CHUNK
            if isinstance(at, int):
                count = min(CHUNK, full_tiles - first)
            lanes = pl.ds(pl.multiple_of(first * LANES, LANES), count * LANES)
            copies.append(remote(
                far_row.at[:, lanes], halo.at[1 - core, :, lanes],
                halo_send.at[part_of, at], halo_recv.at[part_of, at], far_target,
            ))
        return copies

    def start_chunk(at):
        @pl.when(crosses)
        def _():
            for copy in chunk(at):
                copy.start()

    def sent_chunk(at):
        @pl.when(crosses)
        def _():
            for copy in chunk(at):
                copy.wait_send()

    def received_chunk(at):
        @pl.when(crosses)
        def _():
            for copy in chunk(at):
                copy.wait_recv()

    order = [CHUNKS - 1] + list(range(CHUNKS - 1))

    def start_chunks(begin, end):
        for step in range(begin, end):
            start_chunk(order[step])

    start_chunks(0, FIRST)

    lane = iota((8, LANES), 1)

    loads[0].wait()
    loads[1].wait()
    ones = jnp.ones((rows * cols, LANES), BF16)
    sums = [jnp.zeros((8, LANES), F32)] * 4
    for block in range(BLOCKS):
        start = block * LANES
        width = min(LANES, kbuf.shape[2] - start)
        keys = jnp.maximum(kbuf[:, :, start : start + width], 0).reshape(rows * cols, width)
        values = vbuf[:, :, start : start + width].reshape(rows * cols, width)
        contract = (((0,), (0,)), ((), ()))
        if width == LANES:
            both = lax.dot_general(
                keys, jnp.concatenate([values, ones], axis=1), contract, preferred_element_type=F32
            )
            state, key_sum = both[:, :LANES], both[:, LANES:]
        else:
            state = lax.dot_general(keys, values, contract, preferred_element_type=F32)
            state = jnp.concatenate([state, jnp.zeros((width, LANES - width), F32)], axis=1)
            key_sum = lax.dot_general(keys, ones, contract, preferred_element_type=F32)
        heads = width // HEAD_DIM
        for group in range(4):
            tile = jnp.zeros((8, LANES), F32)
            for h in range(heads):
                at = slice(h * HEAD_DIM + group * 8, h * HEAD_DIM + group * 8 + 8)
                tile = jnp.where(lax.div(lane, HEAD_DIM) == h, state[at], tile)
                sums[group] = jnp.where(lane == block * 4 + h, key_sum[at], sums[group])
            part[slot(block * 4 + group)] = tile
    for group in range(4):
        part[slot(BLOCKS * 4 + group)] = sums[group]
        part[slot(BLOCKS * 4 + 4 + group)] = jnp.zeros((8, LANES), F32)
    for quarter in range(8):
        for unused in range(USED, QUARTER):
            part[quarter * QUARTER + unused] = jnp.zeros((8, LANES), F32)

    def quarter(at, size=USED):
        return pl.ds(core * HALF + at * QUARTER, size)

    def share(at):
        return pl.ds(core * HALF + x * QUARTER + at * SHARE, SHARE)

    def ring(at, d, n):
        return lax.rem(at + d + n, n)

    mine_half, other_half = pl.ds(core * HALF, HALF), pl.ds((1 - core) * HALF, HALF)
    mine_x, mine_y = quarter(x), share(y)
    add_core = remote(part.at[other_half], recv_core, core_send.at[0], core_recv.at[0], core_mate)
    add_x, add_y, add_z, give_x, give_y, get_x, get_y = [], [], [], [], [], [], []
    for d in range(1, 4):
        a, b = d - 1, d + 2
        add_x.append(remote(part.at[quarter(ring(x, d, 4))], recv_x.at[a], x_send.at[a], x_recv.at[a], x_mates[a]))
        add_y.append(remote(part.at[share(ring(y, d, 4))], recv_y.at[a], y_send.at[a], y_recv.at[a], y_mates[a]))
        give_x.append(remote(total.at[mine_x], total.at[mine_x], x_send.at[b], x_recv.at[b], x_mates[a]))
        give_y.append(remote(total.at[mine_y], total.at[mine_y], y_send.at[b], y_recv.at[b], y_mates[a]))
        from_x, from_y = quarter(ring(x, -d, 4)), share(ring(y, -d, 4))
        get_x.append(remote(total.at[from_x], total.at[from_x], x_send.at[b], x_recv.at[b], x_mates[a]))
        get_y.append(remote(total.at[from_y], total.at[from_y], y_send.at[b], y_recv.at[b], y_mates[a]))
    for d in range(1, 8):
        add_z.append(remote(part.at[mine_y], recv_z.at[d - 1], z_send.at[d - 1], z_recv.at[d - 1], z_mates[d - 1]))
    give_core = remote(total.at[mine_half], total.at[mine_half], core_send.at[1], core_recv.at[1], core_mate)
    get_core = remote(total.at[other_half], total.at[other_half], core_send.at[1], core_recv.at[1], core_mate)

    def start_all(copies):
        for copy in copies:
            copy.start()

    def receive_all(copies):
        for copy in copies:
            copy.wait_recv()

    def sum_core():
        add_core.wait_recv()
        part[mine_half] = part[mine_half] + recv_core[...]
        start_all(add_x)

    def sum_x():
        receive_all(add_x)
        part[mine_x] = part[mine_x] + recv_x[0] + recv_x[1] + recv_x[2]
        start_all(add_y)

    def sum_y():
        receive_all(add_y)
        part[mine_y] = part[mine_y] + recv_y[0] + recv_y[1] + recv_y[2]
        start_all(add_z)

    def sum_z():
        receive_all(add_z)
        got = part[mine_y]
        for d in range(7):
            got = got + recv_z[d]
        total[mine_y] = got
        start_all(give_y)

    def share_y():
        receive_all(get_y)
        start_all(give_x)

    def share_x():
        receive_all(get_x)
        give_core.start()

    add_core.start()

    loads[2].wait()

    def edge_tile(lanes, width):
        row_id = iota((8, width), 0)
        low = high = jnp.zeros((8, width), F32)
        for r in range(rows):
            first = xbuf[r, 0:16, lanes].astype(F32)[0:1]
            last = xbuf[r, cols - 16 : cols, lanes].astype(F32)[15:16]
            if r in (0, rows - 1):
                place = 0 if r == 0 else 2
                corner_out[place, :, lanes] = first
                corner_out[place + 1, :, lanes] = last
            low = jnp.where(row_id == r, first, low)
            high = jnp.where(row_id == r, last, high)
        send_left[:, lanes] = low.astype(BF16)
        send_right[:, lanes] = high.astype(BF16)

    @pl.loop(0, full_tiles)
    def _(t):
        edge_tile(pl.ds(pl.multiple_of(t * LANES, LANES), LANES), LANES)

    edge_tile(slice(full_tiles * LANES, channels), tail)
    sum_core()
    rest = xbuf[core * (rows - 1), :, full_tiles * LANES :]
    tail_out[...] = jnp.concatenate([rest, jnp.zeros((cols, LANES - tail), BF16)], axis=1)
    far_tail = remote(tail_out, tail_in, mate_send.at[1], mate_recv.at[1], far_target)

    to_left = remote(send_left, right, edge_send.at[0], edge_recv.at[0], (row, col - 1))
    to_right = remote(send_right, left, edge_send.at[1], edge_recv.at[1], (row, col + 1))
    pl.when(has_left)(to_left.start)
    pl.when(has_right)(to_right.start)
    to_corner = [
        remote(corner_out.at[i], corner_in.at[3 - i], corner_send.at[i], corner_recv.at[3 - i], (row + a, col + b))
        for i, _, a, b in diagonals
    ]
    def send_corners():
        for i, there, _, _ in diagonals:
            pl.when(there)(to_corner[i].start)


    def bias_at(lanes, width):
        return bias_row[:, lanes]

    pl.when(crosses)(far_tail.start)

    groups = cols // 8

    def conv(lanes, width, out_rows, out_groups):
        sub = iota((8, width), 0)

        def wide(v):
            return jnp.broadcast_to(v, (8, width))

        weight = []
        for a in range(3):
            taps = wbuf[a, :, lanes].astype(F32)
            weight.append([wide(taps[b : b + 1]) for b in range(3)])
        bias = wide(bias_at(lanes, width))

        def fetch(r):
            source = []
            for at in range(0, cols, 16):
                if r < 0 or r >= rows:
                    pair = halo[int(r >= rows), at : at + 16, lanes]
                else:
                    pair = xbuf[r, at : at + 16, lanes]
                pair = pair.astype(F32)
                source += [pair[:8], pair[8:]]
            return source

        def edge(column, tap, corners):
            middle = column[:, lanes].astype(F32)
            above, below = pltpu.roll(middle, 1, axis=0), pltpu.roll(middle, 7, axis=0)
            if out_rows[0] == 0:
                above = jnp.where(sub == 0, wide(corner_in[corners[0], :, lanes]), above)
                below = jnp.where(sub == 7, wide(corner_in[corners[1], :, lanes]), below)
            return weight[0][tap] * above + weight[1][tap] * middle + weight[2][tap] * below

        if 0 in out_groups:
            low, high = edge(left, 0, (0, 2)), edge(right, 2, (1, 3))
        window = {}
        for r in out_rows:
            window = {a: window[a] if a in window else fetch(a) for a in (r - 1, r, r + 1)}
            before, now, after = window[r - 1], window[r], window[r + 1]

            def tap(b, g):
                return weight[0][b] * before[g] + weight[1][b] * now[g] + weight[2][b] * after[g]

            from_low, from_high = {}, {}
            for g in range(groups):
                if g in out_groups or g + 1 in out_groups:
                    from_low[g] = pltpu.roll(tap(0, g), 1, axis=0)
                if g in out_groups or g - 1 in out_groups:
                    from_high[g] = pltpu.roll(tap(2, g), 7, axis=0)
            if 0 in out_groups:
                from_low[-1], from_high[groups] = wide(low[r : r + 1]), wide(high[r : r + 1])
            yield [
                (tap(1, g) + bias)
                + jnp.where(sub == 0, from_low[g - 1], from_low[g])
                + jnp.where(sub == 7, from_high[g + 1], from_high[g])
                for g in out_groups
            ]

    def gate_tile(lanes, width, where, second=0):
        at = 0
        for sums_of_row in conv(lanes, width, *where):
            for v in sums_of_row:
                half = 0.5 * v
                v = half + half * jnp.tanh(half)
                if width < LANES:
                    v = jnp.concatenate([v, jnp.zeros((8, LANES - width), F32)], axis=1)
                v = pltpu.roll(v, GATE_SHIFT, axis=1)
                gates[second + at] = jnp.where(lane < GATE_SHIFT, prev[at], v)
                prev[at] = v
                at += 1

    def value_tile(lanes, width, where, second=0):
        at = 0
        for r, sums_of_row in zip(where[0], conv(lanes, LANES, *where)):
            for g, v in zip(where[1], sums_of_row):
                out = (v * gates[second + at]).astype(BF16)
                if width == LANES:
                    gbuf[r, 8 * g : 8 * g + 8, lanes] = out
                else:
                    gbuf[r, 8 * g : 8 * g + 8, HID - width : HID] = out[:, :width]
                at += 1

    def tile_at(t):
        return pl.ds(pl.multiple_of(t * LANES, LANES), LANES)

    def first_tile(where):
        for at in range(len(where[0]) * len(where[1])):
            prev[at] = jnp.zeros((8, LANES), F32)
        gate_tile(slice(GATE_TILE * LANES, GATE_TILE * LANES + LANES), LANES, where)

    def some_tiles(where, begin, count, actions=()):
        def one(u, second=0):
            gate_tile(tile_at(u + GATE_TILE + 1), LANES, where, second)
            value_tile(tile_at(u), LANES, where, second)

        pairs = count // 2

        @pl.loop(0, pairs)
        def _(pair):
            for at, action, argument in actions:
                pl.when(pair == at // 2)(functools.partial(action, *argument))
            one(begin + 2 * pair)
            one(begin + 2 * pair + 1, len(where[0]) * len(where[1]))

        if count % 2:
            one(begin + count - 1)

    def last_tile(where):
        gate_tile(slice(full_tiles * LANES, channels), tail, where)
        value_tile(slice(GATE_TILE * LANES, GATE_TILE * LANES + LANES), HID % LANES, where)

    loads[3].wait()
    loads[4].wait()
    for at in range(0, channels, 1024):
        piece = bbuf[at : min(at + 1024, channels)].astype(F32)
        bias_row[:, at : min(at + 1024, channels)] = piece.reshape(1, -1)
    where = (list(range(1, rows - 1)), list(range(1, groups - 1)))
    first_tile(where)
    some_tiles(where, 0, GATE_TILE, [
        (SUM_X_AT, sum_x, ()), (SUM_Y_AT, sum_y, ()), (SUM_Y_AT, send_corners, ()), (SUM_Y_AT, start_chunks, (FIRST, SECOND)),
    ])
    last_tile(where)

    pl.when(has_right)(to_left.wait_recv)
    pl.when(has_left)(to_right.wait_recv)
    where = (list(range(1, rows - 1)), [0, groups - 1])
    first_tile(where)
    some_tiles(where, 0, GATE_TILE, [(SUM_Z_AT, sum_z, ()), (SUM_Z_AT, start_chunks, (SECOND, CHUNKS))])
    last_tile(where)
    share_y()
    store_inner = pltpu.make_async_copy(
        gbuf.at[pl.ds(1, rows - 2)], gated_hbm.at[pl.ds(1, rows - 2)], store_sem.at[0]
    )
    store_inner.start()

    received_chunk(CHUNKS - 1)
    mate_row.wait_recv()

    @pl.when(crosses)
    def _():
        far_tail.wait_recv()
        halo[core, :, full_tiles * LANES :] = tail_in[:, :tail]

    for i, there, _, _ in diagonals:
        pl.when(there)(to_corner[3 - i].wait_recv)
    where = ([0, rows - 1], list(range(groups)))
    first_tile(where)

    @pl.loop(0, CHUNKS - 1)
    def _(at):
        pl.when(at == SHARE_X_AT)(share_x)
        received_chunk(at)
        some_tiles(where, at * CHUNK, CHUNK)

    some_tiles(where, (CHUNKS - 1) * CHUNK, GATE_TILE - (CHUNKS - 1) * CHUNK)
    last_tile(where)
    store_first = pltpu.make_async_copy(gbuf.at[0], gated_hbm.at[0], store_sem.at[2])
    store_last = pltpu.make_async_copy(gbuf.at[rows - 1], gated_hbm.at[rows - 1], store_sem.at[3])
    store_first.start()
    store_last.start()
    get_core.wait_recv()
    store_state = pltpu.make_async_copy(total, state_hbm, store_sem.at[1])
    store_state.start()

    for at in order:
        sent_chunk(at)
    mate_row.wait_send()
    pl.when(crosses)(far_tail.wait_send)
    pl.when(has_left)(to_left.wait_send)
    pl.when(has_right)(to_right.wait_send)
    for i, there, _, _ in diagonals:
        pl.when(there)(to_corner[i].wait_send)
    for copy in [add_core, give_core] + add_x + add_y + add_z + give_y + give_x:
        copy.wait_send()
    for store in [store_inner, store_state, store_first, store_last]:
        store.wait()


def mix(keys, values, features, conv_weight, conv_bias):
    rows, cols, channels = features.shape
    width = keys.shape[2]
    sem = pltpu.SemaphoreType.DMA
    tiles = lambda *lead: pltpu.VMEM(lead + (8, LANES), F32)
    anywhere = pl.BlockSpec(memory_space=pl.ANY)
    return pl.pallas_call(
        mix_kernel,
        name="mix",
        out_shape=(
            jax.ShapeDtypeStruct((TILES, 8, LANES), F32),
            jax.ShapeDtypeStruct((rows, cols, HID), BF16),
        ),
        in_specs=[pl.BlockSpec(memory_space=pltpu.HBM)] * 5,
        out_specs=[anywhere] * 2,
        scratch_shapes=[
            pltpu.VMEM((rows, cols, width), BF16),
            pltpu.VMEM((rows, cols, width), BF16),
            pltpu.VMEM((rows, cols, channels), BF16),
            pltpu.VMEM((3, 3, channels), BF16),
            pltpu.VMEM((channels,), BF16),
            pltpu.VMEM((1, channels), F32),
            pltpu.VMEM((rows, cols, HID), BF16),
            pltpu.VMEM((2, cols, channels), BF16),
            pltpu.VMEM((rows, channels), BF16),
            pltpu.VMEM((rows, channels), BF16),
            pltpu.VMEM((rows, channels), BF16),
            pltpu.VMEM((rows, channels), BF16),
            pltpu.VMEM((4, 1, channels), F32),
            pltpu.VMEM((4, 1, channels), F32),
            pltpu.VMEM((cols, LANES), BF16),
            pltpu.VMEM((cols, LANES), BF16),
            tiles((rows - 2) * cols // 8),
            tiles((rows - 2) * cols // 8),
            tiles(TILES),
            tiles(HALF),
            tiles(3, USED),
            tiles(7, SHARE),
            tiles(3, SHARE),
            tiles(TILES),
            sem((5,)), sem((4,)), sem((2, CHUNKS)), sem((2, CHUNKS)), sem((2,)), sem((2,)),
            sem((2,)), sem((2,)), sem((4,)), sem((4,)),
            sem((2,)), sem((2,)), sem((6,)), sem((6,)), sem((7,)), sem((7,)), sem((6,)), sem((6,)),
        ],
        compiler_params=pltpu.CompilerParams(
            collective_id=0, has_side_effects=True, vmem_limit_bytes=48 << 20
        ),
        cost_estimate=pl.CostEstimate(flops=100_000_000, bytes_accessed=12_000_000, transcendentals=1_500_000),
    )(keys, values, features, conv_weight, conv_bias)


def attend_kernel(q_hbm, state, mixed_hbm, attended_hbm, gated_hbm, qbuf, abuf, matrix, sem):
    rows, cols, width = qbuf.shape
    move = pltpu.make_async_copy(mixed_hbm, gated_hbm, sem.at[0])
    load = pltpu.make_async_copy(q_hbm, qbuf, sem.at[1])
    load.start()
    move.start()

    lane = iota((HEAD_DIM, LANES), 1)
    head_of_lane = lax.div(lane, HEAD_DIM)

    def split(v):
        high = v.astype(BF16)
        return high, (v - high.astype(F32)).astype(BF16)

    def rows_of(block):
        return jnp.concatenate([state[slot(block * 4 + group)] for group in range(4)], axis=0)

    sum_high, sum_low = split(rows_of(BLOCKS))

    def block_diagonal(v):
        v = v.astype(F32)
        return jnp.concatenate([jnp.where(head_of_lane == h, v, 0.0) for h in range(4)], axis=0).astype(BF16)

    def build(block):
        high, low = split(rows_of(block))
        picks = (iota((LANES, LANES), 0) == block * 4 + lax.div(iota((LANES, LANES), 1), HEAD_DIM))
        picks = picks.astype(F32).astype(BF16)
        key_high = jnp.dot(sum_high, picks, preferred_element_type=F32)
        key_low = jnp.dot(sum_low, picks, preferred_element_type=F32)
        top = jnp.concatenate([block_diagonal(high), block_diagonal(key_high)], axis=1)
        bottom = jnp.concatenate([block_diagonal(low), block_diagonal(key_low)], axis=1)
        matrix[block] = jnp.concatenate([top, bottom], axis=0)

    for block in range(BLOCKS):
        build(block)
    load.wait()
    for block in range(BLOCKS):
        start = block * LANES
        size = min(LANES, width - start)
        queries = jnp.maximum(qbuf[:, :, start : start + size], 0).reshape(rows * cols, size)
        if size < LANES:
            queries = jnp.concatenate([queries, jnp.zeros((rows * cols, LANES - size), BF16)], axis=1)
        both = jnp.dot(jnp.concatenate([queries, queries], axis=1), matrix[block], preferred_element_type=F32)
        out = (both[:, :LANES] / (both[:, LANES:] + 1e-15)).astype(BF16).reshape(rows, cols, LANES)
        abuf[:, :, start : start + size] = out[:, :, :size]
    store = pltpu.make_async_copy(abuf, attended_hbm, sem.at[2])
    store.start()
    store.wait()
    move.wait()


def attend(queries, state, mixed):
    anywhere = pl.BlockSpec(memory_space=pl.ANY)
    return pl.pallas_call(
        attend_kernel,
        name="attend",
        out_shape=(
            jax.ShapeDtypeStruct(queries.shape, BF16),
            jax.ShapeDtypeStruct(mixed.shape, BF16),
        ),
        in_specs=[anywhere, pl.BlockSpec(memory_space=pltpu.VMEM), anywhere],
        out_specs=[anywhere] * 2,
        scratch_shapes=[
            pltpu.VMEM(queries.shape, BF16),
            pltpu.VMEM(queries.shape, BF16),
            pltpu.VMEM((BLOCKS, 2 * LANES, 2 * LANES), BF16),
            pltpu.SemaphoreType.DMA((3,)),
        ],
        compiler_params=pltpu.CompilerParams(vmem_limit_bytes=32 << 20),
        cost_estimate=pl.CostEstimate(flops=600_000_000, bytes_accessed=8_000_000, transcendentals=0),
    )(queries, state, mixed)


def on_device(queries, keys, values, features, conv_weight, conv_bias):
    hold = functools.partial(pltpu.with_memory_space_constraint, memory_space=pltpu.HBM)
    keys, values, conv_weight = hold(keys), hold(values), hold(conv_weight)
    state, mixed = mix(keys, values, features, conv_weight, conv_bias)
    return attend(queries, state, mixed)


def solution(mesh):
    return jax.shard_map(
        on_device,
        mesh=mesh,
        in_specs=(
            P("row", "col", None),
            P("row", "col", None),
            P("row", "col", None),
            P("row", "col", None),
            P(),
            P(),
        ),
        out_specs=(P("row", "col", None), P("row", "col", None)),
        check_vma=False,
    )
```
